32 devices in a mesh: parts: 2 (over x), inner: 16 (over z, y, core).
Axes of the slice: x: 2, y: 2, z: 4, core: 2. Of those that a mesh axis runs over, the one named last changes fastest.
Arguments:
- queries: bfloat16 [768, 128], P(('parts', 'inner')), parts along dimension 0, may hold values from -150 to 150
- new_kv: bfloat16 [2, 3, 4, 1024], P(None, None, 'parts'), parts along dimension 2, may hold values from -6 to 6
- cache_keys: bfloat16 [65536, 1024], P(('parts', 'inner')), parts along dimension 0, may hold values from -6 to 6
- cache_values: bfloat16 [65536, 1024], P(('parts', 'inner')), parts along dimension 0, may hold values from -6 to 6
- context_lengths: int32 [4], P('parts'), parts along dimension 0, may hold values from 128 to 24576, as said below
- block_table: int32 [512], P(('parts', 'inner')), parts along dimension 0, may hold values from -1 to 383, as said below
Outputs:
- attended: bfloat16 [768, 128], P(('parts', 'inner')), parts along dimension 0
The draws below stay inside these ranges and needn't reach their ends.
There are 2 independent parts, one for each index of `parts`. The reference program is written for one: setup_inputs(seed, part) draws one part's arguments, and reference() takes and returns one part's arrays. A program takes and returns all parts, laid end to end along the dimension named above; each array names one. Nothing has to cross between parts.
Inputs may be any that keep to these rules, and one draw needn't show every extreme that they name: `context_lengths`: the last sequence holds exactly 24576 cached tokens, the others fewer. `block_table`: every logical block j < ceil(context_lengths[s] / 128) of every sequence s appears exactly once; all other entries are -1; blocks are placed on devices at random.
All inputs are finite; a program needn't handle non-finite values.
Results may differ from the reference program's by a relative error of at most 0.0095.
Values may be sent and summed in bfloat16 or wider, within the bound.
A program may use at most 64 MiB of HBM per device.

```python
import jax
import jax.numpy as jnp
from jax import lax

HEADS = 64
KV_HEADS = 8
HEAD_DIM = 128
SEQS = 2
BLK_DEV = 16
BLK = 128
STEPS = 3
BLOCKS = 256
MAXBLK = 192
ROWS = 384
N_INNER = 16


def draw_queries(key, part):
    key_one = jax.random.fold_in(jax.random.fold_in(key, 11), 0)
    values = jnp.clip(jax.random.normal(key_one, (ROWS, HEAD_DIM), jnp.float32) * 2.5, -15.0, 15.0)
    return values.astype(jnp.bfloat16)


def layout(key):
    base = jax.random.fold_in(key, 29)
    key_one = jax.random.fold_in(base, 0)
    key_three = jax.random.fold_in(base, 2)
    spare_cap = (BLOCKS - MAXBLK) // (SEQS - 1)
    others = jax.random.randint(key_one, (SEQS,), BLK, spare_cap * BLK + 1)
    lengths = jnp.where(jnp.arange(SEQS) == SEQS - 1, MAXBLK * BLK, others).astype(jnp.int32)
    counts = (lengths + BLK - 1) // BLK
    ends = jnp.cumsum(counts)
    starts = ends - counts
    index = jnp.arange(BLOCKS, dtype=jnp.int32)
    owner = jnp.sum((index[:, None] >= ends[None, :]).astype(jnp.int32), axis=1)
    owner_safe = jnp.minimum(owner, SEQS - 1)
    logical = index - starts[owner_safe]
    entries = jnp.where(index < ends[-1], owner_safe * MAXBLK + logical, -1).astype(jnp.int32)
    placing = jax.random.permutation(key_three, BLOCKS)
    table = jnp.zeros((BLOCKS,), jnp.int32).at[placing].set(entries)
    return (lengths, table)


def draw_context_lengths(key, part):
    return layout(key)[0]


def draw_block_table(key, part):
    return layout(key)[1]


def block_scale(own_key, dims, shards, smallest, high):
    factor_of, own = 1.0, jax.random.fold_in(own_key, 6)
    for dim, parts in shards:
        heights = jnp.exp(jax.random.uniform(jax.random.fold_in(own, dim), (parts,), jnp.float32, smallest / len(shards), high / len(shards)))
        factor_of = factor_of * jnp.repeat(heights, dims[dim] // parts).reshape([-1 if axis == dim else 1 for axis in range(len(dims))])
    return factor_of


def gaussian(stream_key, dims, width, reach, cuts=(), held_as=jnp.bfloat16):
    drawn = jax.random.normal(stream_key, dims, jnp.float32) * width
    if len(cuts) > 0:
        drawn = block_scale(stream_key, dims, cuts, -0.22, 0.18) * drawn
    return jnp.clip(drawn, min=-reach, max=reach).astype(held_as)


def setup_inputs(seed: int = 0, part: int = 0) -> dict:
    splits = jax.random.split(jax.random.key(seed), 7)
    own_keys = jax.random.split(jax.random.fold_in(splits[6], part), 7)
    return {
        "queries": draw_queries(jax.random.fold_in(jax.random.fold_in(splits[6], part), 71), part),
        "new_kv": gaussian(own_keys[1], (2, STEPS, SEQS, KV_HEADS * HEAD_DIM), 1.0, 6.0),
        "cache_keys": gaussian(own_keys[2], (BLOCKS * BLK, KV_HEADS * HEAD_DIM), 1.0, 6.0, ((0, 16),)),
        "cache_values": gaussian(own_keys[3], (BLOCKS * BLK, KV_HEADS * HEAD_DIM), 1.0, 6.0, ((0, 16),)),
        "context_lengths": draw_context_lengths(jax.random.fold_in(jax.random.fold_in(splits[6], part), 71), part),
        "block_table": draw_block_table(jax.random.fold_in(jax.random.fold_in(splits[6], part), 71), part),
    }


def reference(queries, new_kv, cache_keys, cache_values, context_lengths, block_table):
    per_kv = HEADS // KV_HEADS
    query_rows = STEPS * per_kv
    inv_root = 1.0 / (HEAD_DIM ** 0.5)
    grouped = queries.astype(jnp.float32).reshape(STEPS, SEQS, KV_HEADS, per_kv, HEAD_DIM)
    grouped = grouped.transpose(1, 2, 0, 3, 4).reshape(SEQS, KV_HEADS, query_rows, HEAD_DIM)
    new_keys = new_kv[0].astype(jnp.float32).reshape(STEPS, SEQS, KV_HEADS, HEAD_DIM)
    new_values = new_kv[1].astype(jnp.float32).reshape(STEPS, SEQS, KV_HEADS, HEAD_DIM)
    new_scores = jnp.einsum("skrd,uskd->skru", grouped, new_keys) * inv_root
    allowed = jnp.arange(STEPS)[None, :] <= (jnp.arange(query_rows) // per_kv)[:, None]
    new_scores = jnp.where(allowed[None, None], new_scores, -jnp.inf)
    key_blocks = cache_keys.reshape(N_INNER, BLK_DEV, BLK, KV_HEADS, HEAD_DIM)
    value_blocks = cache_values.reshape(N_INNER, BLK_DEV, BLK, KV_HEADS, HEAD_DIM)
    tables = block_table.reshape(N_INNER, BLK_DEV)
    seq_ids = jnp.arange(SEQS)

    def block_terms(keys_here, table_here):
        owner = jnp.where(table_here >= 0, table_here // MAXBLK, 0)
        position = (table_here % MAXBLK)[:, None] * BLK + jnp.arange(BLK)[None, :]
        valid = (table_here >= 0)[:, None] & (position < context_lengths[owner][:, None])
        scores = jnp.einsum("bkrd,btkd->bkrt", grouped[owner], keys_here.astype(jnp.float32)) * inv_root
        scores = jnp.where(valid[:, None, None, :], scores, -jnp.inf)
        member = (owner[:, None] == seq_ids[None, :]) & (table_here >= 0)[:, None]
        return scores, owner, member

    def max_step(running, inputs):
        scores, owner, member = block_terms(inputs[0], inputs[1])
        block_max = scores.max(-1)
        seq_max = jnp.where(member[:, :, None, None], block_max[:, None], -jnp.inf).max(0)
        return jnp.maximum(running, seq_max), None

    top, unused = lax.scan(max_step, new_scores.max(-1), (key_blocks, tables))
    weights_new = jnp.exp(new_scores - top[..., None])
    rounded_new = lax.optimization_barrier(weights_new.astype(jnp.bfloat16)).astype(jnp.float32)
    start_denom = weights_new.sum(-1)
    start_numer = jnp.einsum("skru,uskd->skrd", rounded_new, new_values)

    def sum_step(carry, inputs):
        keys_here, values_here, table_here = inputs
        scores, owner, member = block_terms(keys_here, table_here)
        weights = jnp.exp(scores - top[owner][..., None])
        onehot = member.astype(jnp.float32)
        denom = carry[0] + jnp.einsum("bs,bkr->skr", onehot, weights.sum(-1))
        rounded = lax.optimization_barrier(weights.astype(jnp.bfloat16)).astype(jnp.float32)
        mixed = jnp.einsum("bkrt,btkd->bkrd", rounded, values_here.astype(jnp.float32))
        numer = carry[1] + jnp.einsum("bs,bkrd->skrd", onehot, mixed)
        return (denom, numer), None

    totals, unused = lax.scan(sum_step, (start_denom, start_numer), (key_blocks, value_blocks, tables))
    result = totals[1] / totals[0][..., None]
    result = result.reshape(SEQS, KV_HEADS, STEPS, per_kv, HEAD_DIM).transpose(2, 0, 1, 3, 4)
    return result.reshape(STEPS * SEQS * HEADS, HEAD_DIM).astype(jnp.bfloat16)
```

```python
import functools
import math

import jax
import jax.numpy as jnp
from jax import lax
from jax.experimental import pallas as pl
from jax.experimental.pallas import tpu as pltpu
from jax.sharding import PartitionSpec as P

HEADS = 64
KV_HEADS = 8
HEAD_DIM = 128
SEQS = 2
BLK_DEV = 16
BLK = 128
STEPS = 3
PER_KV = HEADS // KV_HEADS
QUERY_ROWS = STEPS * PER_KV
PAIRS = 8
SPLIT = (3, 4, 5, 6)
LOW = -1e30
EXP_SCALE = math.log2(math.e) / HEAD_DIM**0.5
MESH = pl.DeviceIdType.MESH
NT = (((1,), (1,)), ((), ()))


def kernel(
    devices,
    q_hbm, new_hbm, k_hbm, v_hbm, ctx_hbm, table_hbm,
    out_ref,
    k_buf, v_buf, new_buf, ctx_buf, table_buf,
    q_slots, q_flat, q_heads, bias,
    new_k, new_v, own_num, own_stat,
    score_buf, acc, top, den,
    send_num, send_stat, recv_num, recv_stat,
    k_sem, v_sem, small_sem, q_send, q_recv, n_send, n_recv, s_send, s_recv,
):
    me = lax.axis_index("inner")
    rows = q_hbm.shape[0]
    tokens = k_hbm.shape[0]
    max_blocks = 3 * BLK_DEV * devices // (2 * SEQS)

    power = devices & (devices - 1) == 0
    flips, bit = [], 1
    while bit < devices:
        flips.append((bit, bit * (1 - 2 * (me // bit % 2))))
        bit *= 2

    def target(k):
        if power:
            return me + sum(move for bit, move in flips if k & bit)
        return lax.rem(me + k, devices)

    def source(k):
        return target(k) if power else lax.rem(me + devices - k, devices)

    near = range(1, devices)
    far = range(devices - 1, 0, -1)
    barrier = pltpu.get_barrier_semaphore()
    for k in far:
        pl.semaphore_signal(barrier, inc=1, device_id={"inner": target(k)}, device_id_type=MESH)

    small = (
        pltpu.make_async_copy(q_hbm, q_slots.at[me], small_sem.at[0]),
        pltpu.make_async_copy(new_hbm, new_buf, small_sem.at[1]),
        pltpu.make_async_copy(ctx_hbm, ctx_buf, small_sem.at[2]),
        pltpu.make_async_copy(table_hbm, table_buf, small_sem.at[3]),
    )
    for copy in small:
        copy.start()
    loads = []
    for src, dst, sem in ((k_hbm, k_buf, k_sem), (v_hbm, v_buf, v_sem)):
        for g in range(KV_HEADS):
            part = pl.ds(g * HEAD_DIM, HEAD_DIM)
            loads.append(pltpu.make_async_copy(src.at[:, part], dst.at[g], sem.at[g]))
    for copy in loads:
        copy.start()

    def query_copy(k, slot):
        return pltpu.make_async_remote_copy(
            src_ref=q_slots.at[me],
            dst_ref=q_slots.at[slot],
            send_sem=q_send.at[k],
            recv_sem=q_recv.at[k],
            device_id={"inner": target(k)},
            device_id_type=MESH,
        )

    small[0].wait()
    pl.semaphore_wait(barrier, devices - 1)
    for k in far:
        query_copy(k, me).start()
    for copy in small[1:]:
        copy.wait()

    lane = lax.broadcasted_iota(jnp.int32, (8, BLK), 1)
    for b in range(tokens // BLK):
        entry = table_buf[b]
        owner = jnp.where(entry >= 0, entry // max_blocks, -1)
        first = jnp.where(entry >= 0, entry % max_blocks, 0) * BLK
        for s in range(SEQS):
            count = jnp.where(owner == s, ctx_buf[s] - first, 0)
            bias[s, :, b * BLK : (b + 1) * BLK] = jnp.where(lane < count, 0.0, LOW)

    new_k[...] = jnp.zeros_like(new_k)
    new_v[...] = jnp.zeros_like(new_v)
    for u in range(STEPS):
        new_k[u * SEQS : (u + 1) * SEQS, :] = new_buf[0, u].astype(jnp.float32)
        new_v[u * SEQS : (u + 1) * SEQS, :] = new_buf[1, u].astype(jnp.float32)

    def stacked(ref):
        parts = [ref[:, g * HEAD_DIM : (g + 1) * HEAD_DIM] for g in range(KV_HEADS)]
        return jnp.concatenate(parts, axis=0).astype(jnp.bfloat16)

    own_q = q_slots[me]
    score = lax.dot_general(own_q, stacked(new_k), NT, preferred_element_type=jnp.float32)
    row = me * rows + lax.broadcasted_iota(jnp.int32, score.shape, 0)
    col = lax.broadcasted_iota(jnp.int32, score.shape, 1)
    pair = col % PAIRS
    allowed = (
        (pair < STEPS * SEQS)
        & (col // PAIRS == row % HEADS // PER_KV)
        & (pair % SEQS == row // HEADS % SEQS)
        & (pair // SEQS <= row // (HEADS * SEQS))
    )
    score = jnp.where(allowed, score, LOW)
    own_top = score.max(-1, keepdims=True)
    weight = jnp.where(allowed, jnp.exp2((score - own_top) * EXP_SCALE), 0.0)
    own_den = weight.sum(-1, keepdims=True)
    own_num[...] = jnp.dot(
        weight.astype(jnp.bfloat16), stacked(new_v), preferred_element_type=jnp.float32
    )
    eye = lax.broadcasted_iota(jnp.int32, (rows, HEAD_DIM), 0) == lax.broadcasted_iota(
        jnp.int32, (rows, HEAD_DIM), 1
    )

    def as_row(column):
        return jnp.sum(jnp.where(eye, column, 0.0), axis=0, keepdims=True)

    def as_column(line):
        return jnp.sum(jnp.where(eye, line, 0.0), axis=1, keepdims=True)

    own_stat[0:1, :] = as_row(own_top)
    own_stat[1:2, :] = as_row(own_den)

    whole_groups = rows % PER_KV == 0
    if whole_groups:
        for k in range(devices):
            here = me
            if k:
                here = source(k)
                query_copy(k, here).wait_recv()
            for n in range(rows // PER_KV):
                group = here * (rows // PER_KV) + n
                pair = group // KV_HEADS
                at = pair % SEQS * STEPS + pair // SEQS
                q_heads[group % KV_HEADS, at] = q_slots[here, n * PER_KV : (n + 1) * PER_KV, :]
    else:
        for k in near:
            query_copy(k, source(k)).wait_recv()
        for d in range(devices):
            q_flat[d * rows : (d + 1) * rows, :] = q_slots[d].astype(jnp.float32)
        for g in range(KV_HEADS):
            for s in range(SEQS):
                for t in range(STEPS):
                    at = ((t * SEQS + s) * KV_HEADS + g) * PER_KV
                    q_heads[g, s * STEPS + t] = q_flat[at : at + PER_KV, :].astype(jnp.bfloat16)
    for copy in loads:
        copy.wait()

    def result_copies(k, slot):
        dst = target(k)
        return tuple(
            pltpu.make_async_remote_copy(
                src_ref=src.at[dst],
                dst_ref=into.at[slot],
                send_sem=out_sem.at[k],
                recv_sem=in_sem.at[k],
                device_id={"inner": dst},
                device_id_type=MESH,
            )
            for src, into, out_sem, in_sem in (
                (send_num, recv_num, n_send, n_recv),
                (send_stat, recv_stat, s_send, s_recv),
            )
        )

    early = power and whole_groups

    def send_to(d):
        k = 0
        for bit, move in flips:
            here = me // bit % 2
            k = k + bit * (1 - here if d & bit else here)

        @pl.when(me != d)
        def _():
            for src, into, out_sem, in_sem in (
                (send_num, recv_num, n_send, n_recv),
                (send_stat, recv_stat, s_send, s_recv),
            ):
                pltpu.make_async_remote_copy(
                    src_ref=src.at[d],
                    dst_ref=into.at[me],
                    send_sem=out_sem.at[k],
                    recv_sem=in_sem.at[k],
                    device_id={"inner": d},
                    device_id_type=MESH,
                ).start()

    def scores(g):
        score = lax.dot_general(
            q_heads[g].reshape(SEQS * QUERY_ROWS, HEAD_DIM), k_buf[g], NT, preferred_element_type=jnp.float32)
        score = score.reshape(SEQS, STEPS, PER_KV, tokens) + bias[...][:, None]
        score_buf[g % 2] = score
        return score.max(-1, keepdims=True)

    def finish(g, high):
        weight = jnp.exp2((score_buf[g % 2] - high) * EXP_SCALE)
        total = weight.sum(-1, keepdims=True)
        mixed = jnp.dot(
            weight.astype(jnp.bfloat16).reshape(SEQS * QUERY_ROWS, tokens),
            v_buf[g],
            preferred_element_type=jnp.float32,
        )
        for s in range(SEQS):
            for t in range(STEPS):
                at = ((t * SEQS + s) * KV_HEADS + g) * PER_KV
                lo = (s * STEPS + t) * PER_KV
                part = mixed[lo : lo + PER_KV]
                if whole_groups:
                    d, off = at // rows, at % rows
                    send_num[d, off : off + PER_KV, :] = part.astype(jnp.bfloat16)
                    spot = lane == sub + off
                    for which, column in enumerate((high, total)):
                        line = jnp.sum(jnp.where(spot, column[s, t], 0.0), axis=0, keepdims=True)
                        lines[d, which] = lines[d, which] + line if (d, which) in lines else line
                    filled[d] += PER_KV
                    if filled[d] == rows:
                        ready.append(d)
                        send_stat[d, 0:1, :] = lines[d, 0]
                        send_stat[d, 1:2, :] = lines[d, 1]
                else:
                    acc[at : at + PER_KV, :] = part
                    top[at : at + PER_KV, :] = jnp.broadcast_to(high[s, t], part.shape)
                    den[at : at + PER_KV, :] = jnp.broadcast_to(total[s, t], part.shape)

    sub = lax.broadcasted_iota(jnp.int32, (PER_KV, BLK), 0)
    lines, filled, ready = {}, [0] * devices, []
    ahead = scores(0)
    for g in range(KV_HEADS):
        high = ahead
        if g + 1 < KV_HEADS:
            ahead = scores(g + 1)
        finish(g, high)
        if early and g in SPLIT:
            for d in ready:
                send_to(d)
            ready.clear()

    if not whole_groups:
        for d in range(devices):
            part = slice(d * rows, (d + 1) * rows)
            send_num[d] = acc[part, :].astype(jnp.bfloat16)
            send_stat[d, 0:1, :] = as_row(top[part, :])
            send_stat[d, 1:2, :] = as_row(den[part, :])
    if early:
        for d in ready:
            send_to(d)
    else:
        for k in far:
            for copy in result_copies(k, me):
                copy.start()

    for k in near:
        query_copy(k, me).wait_send()
    recv_num[me] = send_num[me]
    recv_stat[me] = send_stat[me]
    for k in near:
        for copy in result_copies(k, me):
            copy.wait_send()
    for k in near:
        for copy in result_copies(k, source(k)):
            copy.wait_recv()

    tops = [own_stat[0:1, :]] + [recv_stat[d, 0:1, :] for d in range(devices)]
    dens = [own_stat[1:2, :]] + [recv_stat[d, 1:2, :] for d in range(devices)]
    high = functools.reduce(jnp.maximum, tops)
    scales = [jnp.exp2((one - high) * EXP_SCALE) for one in tops]
    total = functools.reduce(jnp.add, [a * b for a, b in zip(scales, dens)])
    total = jnp.where(total > 0.0, total, 1.0)
    result = as_column(scales[0] / total) * own_num[...]
    for d in range(devices):
        result = result + as_column(scales[d + 1] / total) * recv_num[d].astype(jnp.float32)
    out_ref[...] = result.astype(out_ref.dtype)


def shards(queries, new_kv, cache_keys, cache_values, context_lengths, block_table):
    devices = lax.axis_size("inner")
    rows = queries.shape[0]
    every = rows * devices
    tokens, width = cache_keys.shape
    dma = pltpu.SemaphoreType.DMA
    f32, bf16 = jnp.float32, jnp.bfloat16
    call = pl.pallas_call(
        functools.partial(kernel, devices),
        out_shape=jax.ShapeDtypeStruct(queries.shape, queries.dtype),
        in_specs=[pl.BlockSpec(memory_space=pltpu.HBM)] * 6,
        out_specs=pl.BlockSpec(memory_space=pltpu.VMEM),
        scratch_shapes=[
            pltpu.VMEM((KV_HEADS, tokens, HEAD_DIM), bf16),
            pltpu.VMEM((KV_HEADS, tokens, HEAD_DIM), bf16),
            pltpu.VMEM(new_kv.shape, bf16),
            pltpu.SMEM(context_lengths.shape, jnp.int32),
            pltpu.SMEM(block_table.shape, jnp.int32),
            pltpu.VMEM((devices, rows, HEAD_DIM), bf16),
            pltpu.VMEM((every, HEAD_DIM), f32),
            pltpu.VMEM((KV_HEADS, SEQS * STEPS, PER_KV, HEAD_DIM), bf16),
            pltpu.VMEM((SEQS, PER_KV, tokens), f32),
            pltpu.VMEM((PAIRS, width), f32),
            pltpu.VMEM((PAIRS, width), f32),
            pltpu.VMEM((rows, HEAD_DIM), f32),
            pltpu.VMEM((2, HEAD_DIM), f32),
            pltpu.VMEM((2, SEQS, STEPS, PER_KV, tokens), f32),
            pltpu.VMEM((every, HEAD_DIM), f32),
            pltpu.VMEM((every, HEAD_DIM), f32),
            pltpu.VMEM((every, HEAD_DIM), f32),
            pltpu.VMEM((devices, rows, HEAD_DIM), bf16),
            pltpu.VMEM((devices, 2, HEAD_DIM), f32),
            pltpu.VMEM((devices, rows, HEAD_DIM), bf16),
            pltpu.VMEM((devices, 2, HEAD_DIM), f32),
            dma((KV_HEADS,)),
            dma((KV_HEADS,)),
            dma((4,)),
        ]
        + [dma((devices,))] * 6,
        compiler_params=pltpu.CompilerParams(
            collective_id=0, has_side_effects=True, vmem_limit_bytes=32 * 1024 * 1024
        ),
        name="paged_decode",
    )
    operands = (queries, new_kv, cache_keys, cache_values, context_lengths, block_table)
    return call(*(pltpu.with_memory_space_constraint(x, pltpu.HBM) for x in operands))


def solution(mesh):
    in_specs = (
        P(("parts", "inner"), None),
        P(None, None, "parts", None),
        P(("parts", "inner"), None),
        P(("parts", "inner"), None),
        P("parts"),
        P(("parts", "inner")),
    )
    out_specs = P(("parts", "inner"), None)
    return jax.shard_map(shards, mesh=mesh, in_specs=in_specs, out_specs=out_specs, check_vma=False)
```

```python
import functools
import math

import jax
import jax.numpy as jnp
from jax import lax
from jax.experimental import pallas as pl
from jax.experimental.pallas import tpu as pltpu
from jax.sharding import PartitionSpec as P

HEADS = 64
KV_HEADS = 8
HEAD_DIM = 128
SEQS = 2
BLK_DEV = 16
BLK = 128
STEPS = 3
PER_KV = HEADS // KV_HEADS
SENDS = (2, 5, 7)
QUERY_ROWS = STEPS * PER_KV
PAIRS = 8
LOW = -1e30
EXP_SCALE = math.log2(math.e) / HEAD_DIM**0.5
MESH = pl.DeviceIdType.MESH
NT = (((1,), (1,)), ((), ()))


def kernel(
    devices,
    q_hbm, new_hbm, k_hbm, v_hbm, ctx_hbm, table_hbm,
    out_ref,
    k_buf, kt_buf, v_buf, new_buf, ctx_buf, table_buf,
    q_own, q_slots, q_flat, q_heads, bias,
    new_k, new_v, own_num, own_stat,
    score_buf, acc, top, den,
    send_msg, recv_msg,
    k_sem, v_sem, small_sem, q_send, q_recv, r_send, r_recv,
):
    me = lax.axis_index("inner")
    rows = q_hbm.shape[0]
    tokens = k_hbm.shape[0]
    max_blocks = 3 * BLK_DEV * devices // (2 * SEQS)

    power = devices & (devices - 1) == 0
    flips, bit = [], 1
    while bit < devices:
        flips.append((bit, bit * (1 - 2 * (me // bit % 2))))
        bit *= 2

    def target(k):
        if power:
            return me + sum(move for bit, move in flips if k & bit)
        return lax.rem(me + k, devices)

    def source(k):
        return target(k) if power else lax.rem(me + devices - k, devices)

    near = range(1, devices)
    far = range(devices - 1, 0, -1)
    load_q = pltpu.make_async_copy(q_hbm, q_own, small_sem.at[0])
    load_q.start()
    barrier = pltpu.get_barrier_semaphore()
    for k in far:
        pl.semaphore_signal(barrier, inc=1, device_id={"inner": target(k)}, device_id_type=MESH)

    small = (
        pltpu.make_async_copy(new_hbm, new_buf, small_sem.at[1]),
        pltpu.make_async_copy(ctx_hbm, ctx_buf, small_sem.at[2]),
        pltpu.make_async_copy(table_hbm, table_buf, small_sem.at[3]),
    )
    for copy in small:
        copy.start()
    loads = []
    for src, dst, sem in ((k_hbm, k_buf, k_sem), (v_hbm, v_buf, v_sem)):
        for g in range(KV_HEADS):
            part = pl.ds(g * HEAD_DIM, HEAD_DIM)
            loads.append(pltpu.make_async_copy(src.at[:, part], dst.at[g], sem.at[g]))
    for copy in loads:
        copy.start()

    def query_copy(k, slot):
        return pltpu.make_async_remote_copy(
            src_ref=q_own,
            dst_ref=q_slots.at[slot],
            send_sem=q_send.at[k],
            recv_sem=q_recv.at[k],
            device_id={"inner": target(k)},
            device_id_type=MESH,
        )

    load_q.wait()
    pl.semaphore_wait(barrier, devices - 1)
    for k in far:
        query_copy(k, me).start()
    q_slots[me] = q_own[...]
    for copy in small:
        copy.wait()

    lane = lax.broadcasted_iota(jnp.int32, (8, BLK), 1)
    for b in range(tokens // BLK):
        entry = table_buf[b]
        owner = jnp.where(entry >= 0, entry // max_blocks, -1)
        first = jnp.where(entry >= 0, entry % max_blocks, 0) * BLK
        for s in range(SEQS):
            count = jnp.where(owner == s, ctx_buf[s] - first, 0)
            bias[s, :, b * BLK : (b + 1) * BLK] = jnp.where(lane < count, 0.0, LOW)

    new_k[...] = jnp.zeros_like(new_k)
    new_v[...] = jnp.zeros_like(new_v)
    for u in range(STEPS):
        new_k[u * SEQS : (u + 1) * SEQS, :] = new_buf[0, u].astype(jnp.float32)
        new_v[u * SEQS : (u + 1) * SEQS, :] = new_buf[1, u].astype(jnp.float32)

    def stacked(ref):
        parts = [ref[:, g * HEAD_DIM : (g + 1) * HEAD_DIM] for g in range(KV_HEADS)]
        return jnp.concatenate(parts, axis=0).astype(jnp.bfloat16)

    own_q = q_own[...]
    score = lax.dot_general(own_q, stacked(new_k), NT, preferred_element_type=jnp.float32)
    row = me * rows + lax.broadcasted_iota(jnp.int32, score.shape, 0)
    col = lax.broadcasted_iota(jnp.int32, score.shape, 1)
    pair = col % PAIRS
    allowed = (
        (pair < STEPS * SEQS)
        & (col // PAIRS == row % HEADS // PER_KV)
        & (pair % SEQS == row // HEADS % SEQS)
        & (pair // SEQS <= row // (HEADS * SEQS))
    )
    score = jnp.where(allowed, score, LOW)
    own_top = score.max(-1, keepdims=True)
    weight = jnp.where(allowed, jnp.exp2((score - own_top) * EXP_SCALE), 0.0)
    own_den = weight.sum(-1, keepdims=True)
    own_num[...] = jnp.dot(
        weight.astype(jnp.bfloat16), stacked(new_v), preferred_element_type=jnp.float32
    )
    eye = lax.broadcasted_iota(jnp.int32, (rows, HEAD_DIM), 0) == lax.broadcasted_iota(
        jnp.int32, (rows, HEAD_DIM), 1
    )

    def as_row(column):
        return jnp.sum(jnp.where(eye, column, 0.0), axis=0, keepdims=True)

    def as_column(line):
        return jnp.sum(jnp.where(eye, line, 0.0), axis=1, keepdims=True)

    own_stat[0:1, :] = as_row(own_top)
    own_stat[1:2, :] = as_row(own_den)

    for copy in loads[:KV_HEADS]:
        copy.wait()
    for g in range(KV_HEADS):
        kt_buf[g] = k_buf[g].T
    for copy in loads[KV_HEADS:]:
        copy.wait()
    for k in near:
        query_copy(k, source(k)).wait_recv()

    whole_groups = rows % PER_KV == 0
    early = power and whole_groups
    if not whole_groups:
        for d in range(devices):
            q_flat[d * rows : (d + 1) * rows, :] = q_slots[d].astype(jnp.float32)

    def gather(g):
        for s in range(SEQS):
            for t in range(STEPS):
                at = ((t * SEQS + s) * KV_HEADS + g) * PER_KV
                if whole_groups:
                    d, off = at // rows, at % rows
                    q_heads[g, s * STEPS + t] = q_slots[d, off : off + PER_KV, :]
                else:
                    q_heads[g, s * STEPS + t] = q_flat[at : at + PER_KV, :].astype(jnp.bfloat16)

    def result_copy(k, src, dst, slot):
        return pltpu.make_async_remote_copy(
            src_ref=send_msg.at[src],
            dst_ref=recv_msg.at[slot],
            send_sem=r_send.at[k],
            recv_sem=r_recv.at[k],
            device_id={"inner": dst},
            device_id_type=MESH,
        )

    def send_to(d):
        k = 0
        for bit, move in flips:
            here = me // bit % 2
            k = k + bit * (1 - here if d & bit else here)
        result_copy(k, d, jnp.where(me == d, target(1), d), jnp.where(me == d, devices, me)).start()

    stat_row = (rows + 7) // 8 * 8
    deep = lax.broadcasted_iota(jnp.int32, (8, HEAD_DIM), 0)

    def put_stats(d, high, total):
        block = jnp.zeros((8, HEAD_DIM), jnp.float32)
        for n, line in enumerate((high, total)):
            for m in range(3):
                part = line.astype(jnp.bfloat16).astype(jnp.float32)
                block = jnp.where(deep == 3 * n + m, part, block)
                line = line - part
        send_msg[d, stat_row : stat_row + 8, :] = block.astype(jnp.bfloat16)

    def message(ref, slot):
        block = ref[slot, stat_row : stat_row + 8, :].astype(jnp.float32)
        high = block[0:1] + block[1:2] + block[2:3]
        total = block[3:4] + block[4:5] + block[5:6]
        return high, total, ref[slot, 0:rows, :]

    def scores(g):
        gather(g)
        score = jnp.dot(
            q_heads[g].reshape(SEQS * QUERY_ROWS, HEAD_DIM), kt_buf[g], preferred_element_type=jnp.float32
        )
        score = score.reshape(SEQS, STEPS, PER_KV, tokens) + bias[...][:, None]
        score_buf[g % 2] = score
        return score.max(-1, keepdims=True)

    def finish(g, high):
        weight = jnp.exp2((score_buf[g % 2] - high) * EXP_SCALE)
        total = weight.sum(-1, keepdims=True)
        mixed = jnp.dot(
            weight.astype(jnp.bfloat16).reshape(SEQS * QUERY_ROWS, tokens),
            v_buf[g],
            preferred_element_type=jnp.float32,
        )
        for s in range(SEQS):
            for t in range(STEPS):
                at = ((t * SEQS + s) * KV_HEADS + g) * PER_KV
                lo = (s * STEPS + t) * PER_KV
                part = mixed[lo : lo + PER_KV]
                if whole_groups:
                    d, off = at // rows, at % rows
                    send_msg[d, off : off + PER_KV, :] = part.astype(jnp.bfloat16)
                    spot = lane == sub + off
                    for which, column in enumerate((high, total)):
                        lines[d, which] = jnp.where(spot, column[s, t], lines.get((d, which), 0.0))
                    filled[d] += PER_KV
                    if filled[d] == rows:
                        ready.append(d)
                        put_stats(d, *(lines[d, n].sum(0, keepdims=True) for n in range(2)))
                else:
                    acc[at : at + PER_KV, :] = part
                    top[at : at + PER_KV, :] = jnp.broadcast_to(high[s, t], part.shape)
                    den[at : at + PER_KV, :] = jnp.broadcast_to(total[s, t], part.shape)

    sub = lax.broadcasted_iota(jnp.int32, (PER_KV, BLK), 0)
    lines, filled, ready = {}, [0] * devices, []
    ahead = scores(0)
    for g in range(KV_HEADS):
        high = ahead
        if g + 1 < KV_HEADS:
            ahead = scores(g + 1)
        finish(g, high)
        for d in sorted(ready) if early and g in SENDS else ():
            send_to(d)
            ready.remove(d)

    if not whole_groups:
        for d in range(devices):
            part = slice(d * rows, (d + 1) * rows)
            send_msg[d, 0:rows, :] = acc[part, :].astype(jnp.bfloat16)
            put_stats(d, as_row(top[part, :]), as_row(den[part, :]))
    if not early:
        for k in far:
            result_copy(k, target(k), target(k), me).start()

    def merge(parts):
        high = functools.reduce(jnp.maximum, [top for top, _, _ in parts])
        scales = [jnp.exp2((top - high) * EXP_SCALE) for top, _, _ in parts]
        total = functools.reduce(jnp.add, [a * den for a, (_, den, _) in zip(scales, parts)])
        return high, scales, total

    def weighted(scales, parts):
        terms = [as_column(a) * num.astype(jnp.float32) for a, (_, _, num) in zip(scales, parts)]
        return functools.reduce(jnp.add, terms)

    def received(ks):
        for k in ks:
            result_copy(k, 0, target(k), source(k)).wait_recv()
        return [message(recv_msg, source(k)) for k in ks]

    for k in near:
        query_copy(k, me).wait_send()
    last = devices - devices // 4
    parts = [
        (own_stat[0:1, :], own_stat[1:2, :], own_num[...]),
        message(send_msg, me),
    ] + received(range(1, last))
    high, scales, total = merge(parts)
    parts = [(high, total, weighted(scales, parts))] + received(range(last, devices))
    high, scales, total = merge(parts)
    total = jnp.where(total > 0.0, total, 1.0)
    result = weighted([a / total for a in scales], parts)
    for k in near:
        result_copy(k, 0, target(k), me).wait_send()
    if early:
        spare = result_copy(0, 0, target(1), devices)
        spare.wait_send()
        spare.wait_recv()
    out_ref[...] = result.astype(out_ref.dtype)


def shards(queries, new_kv, cache_keys, cache_values, context_lengths, block_table):
    devices = lax.axis_size("inner")
    rows = queries.shape[0]
    every = rows * devices
    deep = ((rows + 7) // 8 * 8 + 8 + 15) // 16 * 16
    tokens, width = cache_keys.shape
    dma = pltpu.SemaphoreType.DMA
    f32, bf16 = jnp.float32, jnp.bfloat16
    call = pl.pallas_call(
        functools.partial(kernel, devices),
        out_shape=jax.ShapeDtypeStruct(queries.shape, queries.dtype),
        in_specs=[pl.BlockSpec(memory_space=pltpu.HBM)] * 6,
        out_specs=pl.BlockSpec(memory_space=pltpu.VMEM),
        scratch_shapes=[
            pltpu.VMEM((KV_HEADS, tokens, HEAD_DIM), bf16),
            pltpu.VMEM((KV_HEADS, HEAD_DIM, tokens), bf16),
            pltpu.VMEM((KV_HEADS, tokens, HEAD_DIM), bf16),
            pltpu.VMEM(new_kv.shape, bf16),
            pltpu.SMEM(context_lengths.shape, jnp.int32),
            pltpu.SMEM(block_table.shape, jnp.int32),
            pltpu.VMEM((rows, HEAD_DIM), bf16),
            pltpu.VMEM((devices, rows, HEAD_DIM), bf16),
            pltpu.VMEM((every, HEAD_DIM), f32),
            pltpu.VMEM((KV_HEADS, SEQS * STEPS, PER_KV, HEAD_DIM), bf16),
            pltpu.VMEM((SEQS, PER_KV, tokens), f32),
            pltpu.VMEM((PAIRS, width), f32),
            pltpu.VMEM((PAIRS, width), f32),
            pltpu.VMEM((rows, HEAD_DIM), f32),
            pltpu.VMEM((2, HEAD_DIM), f32),
            pltpu.VMEM((2, SEQS, STEPS, PER_KV, tokens), f32),
            pltpu.VMEM((every, HEAD_DIM), f32),
            pltpu.VMEM((every, HEAD_DIM), f32),
            pltpu.VMEM((every, HEAD_DIM), f32),
            pltpu.VMEM((devices, deep, HEAD_DIM), bf16),
            pltpu.VMEM((devices + 1, deep, HEAD_DIM), bf16),
            dma((KV_HEADS,)),
            dma((KV_HEADS,)),
            dma((4,)),
        ]
        + [dma((devices,))] * 4,
        compiler_params=pltpu.CompilerParams(
            collective_id=0, has_side_effects=True, vmem_limit_bytes=32 * 1024 * 1024
        ),
        name="paged_decode",
    )
    operands = (queries, new_kv, cache_keys, cache_values, context_lengths, block_table)
    return call(*(pltpu.with_memory_space_constraint(x, pltpu.HBM) for x in operands))


def solution(mesh):
    in_specs = (
        P(("parts", "inner"), None),
        P(None, None, "parts", None),
        P(("parts", "inner"), None),
        P(("parts", "inner"), None),
        P("parts"),
        P(("parts", "inner")),
    )
    out_specs = P(("parts", "inner"), None)
    return jax.shard_map(shards, mesh=mesh, in_specs=in_specs, out_specs=out_specs, check_vma=False)
```

```python
import functools
import math

import jax
import jax.numpy as jnp
from jax import lax
from jax.experimental import pallas as pl
from jax.experimental.pallas import tpu as pltpu
from jax.sharding import PartitionSpec as P

HEADS = 64
KV_HEADS = 8
HEAD_DIM = 128
SEQS = 2
BLK_DEV = 16
BLK = 128
STEPS = 3
PER_KV = HEADS // KV_HEADS
SENDS = (2, 5, 7)
QUERY_ROWS = STEPS * PER_KV
PAIRS = 8
LOW = -1e30
EXP_SCALE = math.log2(math.e) / HEAD_DIM**0.5
MESH = pl.DeviceIdType.MESH
NT = (((1,), (1,)), ((), ()))


def kernel(
    devices,
    q_hbm, new_hbm, k_hbm, v_hbm, ctx_hbm, table_hbm,
    out_ref,
    kv_buf, kt_buf, new_buf, ctx_buf, table_buf,
    q_own, q_slots, q_flat, q_heads, bias,
    new_k, new_v, own_num, own_stat,
    score_buf, acc, top, den,
    send_msg, recv_msg,
    load_sem, q_send, q_recv, r_send, r_recv,
):
    me = lax.axis_index("inner")
    rows = q_hbm.shape[0]
    tokens = k_hbm.shape[0]
    max_blocks = 3 * BLK_DEV * devices // (2 * SEQS)

    power = devices & (devices - 1) == 0
    flips, bit = [], 1
    while bit < devices:
        flips.append((bit, bit * (1 - 2 * (me // bit % 2))))
        bit *= 2

    def target(k):
        if power:
            return me + sum(move for bit, move in flips if k & bit)
        return lax.rem(me + k, devices)

    def source(k):
        return target(k) if power else lax.rem(me + devices - k, devices)

    near = range(1, devices)
    far = range(devices - 1, 0, -1)
    load_q = pltpu.make_async_copy(q_hbm, q_own, load_sem.at[0])
    load_q.start()
    barrier = pltpu.get_barrier_semaphore()
    for k in far:
        pl.semaphore_signal(barrier, inc=1, device_id={"inner": target(k)}, device_id_type=MESH)

    small = (
        pltpu.make_async_copy(new_hbm, new_buf, load_sem.at[1]),
        pltpu.make_async_copy(ctx_hbm, ctx_buf, load_sem.at[2]),
        pltpu.make_async_copy(table_hbm, table_buf, load_sem.at[3]),
    )
    for copy in small:
        copy.start()
    loads = []
    for n, src in enumerate((k_hbm, v_hbm)):
        for g in range(KV_HEADS):
            part = pl.ds(g * HEAD_DIM, HEAD_DIM)
            loads.append(pltpu.make_async_copy(src.at[:, part], kv_buf.at[n, g], load_sem.at[4]))
    for copy in loads:
        copy.start()

    def query_copy(k, slot):
        return pltpu.make_async_remote_copy(
            src_ref=q_own,
            dst_ref=q_slots.at[slot],
            send_sem=q_send.at[0],
            recv_sem=q_recv.at[0],
            device_id={"inner": target(k)},
            device_id_type=MESH,
        )

    load_q.wait()
    pl.semaphore_wait(barrier, devices - 1)
    for k in far:
        query_copy(k, me).start()
    q_slots[me] = q_own[...]
    for copy in small:
        copy.wait()

    lane = lax.broadcasted_iota(jnp.int32, (8, BLK), 1)
    for b in range(tokens // BLK):
        entry = table_buf[b]
        owner = jnp.where(entry >= 0, entry // max_blocks, -1)
        first = jnp.where(entry >= 0, entry % max_blocks, 0) * BLK
        for s in range(SEQS):
            count = jnp.where(owner == s, ctx_buf[s] - first, 0)
            bias[s, :, b * BLK : (b + 1) * BLK] = jnp.where(lane < count, 0.0, LOW)

    new_k[...] = jnp.zeros_like(new_k)
    new_v[...] = jnp.zeros_like(new_v)
    for u in range(STEPS):
        new_k[u * SEQS : (u + 1) * SEQS, :] = new_buf[0, u].astype(jnp.float32)
        new_v[u * SEQS : (u + 1) * SEQS, :] = new_buf[1, u].astype(jnp.float32)

    def stacked(ref):
        parts = [ref[:, g * HEAD_DIM : (g + 1) * HEAD_DIM] for g in range(KV_HEADS)]
        return jnp.concatenate(parts, axis=0).astype(jnp.bfloat16)

    own_q = q_own[...]
    score = lax.dot_general(own_q, stacked(new_k), NT, preferred_element_type=jnp.float32)
    row = me * rows + lax.broadcasted_iota(jnp.int32, score.shape, 0)
    col = lax.broadcasted_iota(jnp.int32, score.shape, 1)
    pair = col % PAIRS
    allowed = (
        (pair < STEPS * SEQS)
        & (col // PAIRS == row % HEADS // PER_KV)
        & (pair % SEQS == row // HEADS % SEQS)
        & (pair // SEQS <= row // (HEADS * SEQS))
    )
    score = jnp.where(allowed, score, LOW)
    own_top = score.max(-1, keepdims=True)
    weight = jnp.where(allowed, jnp.exp2((score - own_top) * EXP_SCALE), 0.0)
    own_den = weight.sum(-1, keepdims=True)
    own_num[...] = jnp.dot(
        weight.astype(jnp.bfloat16), stacked(new_v), preferred_element_type=jnp.float32
    )
    eye = lax.broadcasted_iota(jnp.int32, (rows, HEAD_DIM), 0) == lax.broadcasted_iota(
        jnp.int32, (rows, HEAD_DIM), 1
    )

    def as_row(column):
        return jnp.sum(jnp.where(eye, column, 0.0), axis=0, keepdims=True)

    def as_column(line):
        return jnp.sum(jnp.where(eye, line, 0.0), axis=1, keepdims=True)

    own_stat[0:1, :] = as_row(own_top)
    own_stat[1:2, :] = as_row(own_den)

    def together(ref, count, out_sem, in_sem):
        part = ref.at[pl.ds(0, count)]
        return pltpu.make_async_remote_copy(
            src_ref=part,
            dst_ref=part,
            send_sem=out_sem,
            recv_sem=in_sem,
            device_id={"inner": target(1)},
            device_id_type=MESH,
        )

    pltpu.make_async_copy(kv_buf, kv_buf, load_sem.at[4]).wait()
    for g in range(KV_HEADS):
        kt_buf[g] = kv_buf[0, g].T
    all_queries = together(q_slots, devices - 1, q_send.at[0], q_recv.at[0])
    all_queries.wait_recv()

    whole_groups = rows % PER_KV == 0
    early = power and whole_groups
    if not whole_groups:
        for d in range(devices):
            q_flat[d * rows : (d + 1) * rows, :] = q_slots[d].astype(jnp.float32)

    def gather(g):
        for s in range(SEQS):
            for t in range(STEPS):
                at = ((t * SEQS + s) * KV_HEADS + g) * PER_KV
                if whole_groups:
                    d, off = at // rows, at % rows
                    q_heads[g, s * STEPS + t] = q_slots[d, off : off + PER_KV, :]
                else:
                    q_heads[g, s * STEPS + t] = q_flat[at : at + PER_KV, :].astype(jnp.bfloat16)

    last = devices - devices // 4

    def result_copy(src, dst, slot, late):
        return pltpu.make_async_remote_copy(
            src_ref=send_msg.at[src],
            dst_ref=recv_msg.at[slot],
            send_sem=r_send.at[0],
            recv_sem=r_recv.at[late],
            device_id={"inner": dst},
            device_id_type=MESH,
        )

    def send_to(d):
        k = 0
        for bit, move in flips:
            here = me // bit % 2
            k = k + bit * (1 - here if d & bit else here)
        own = me == d
        dst, slot = jnp.where(own, target(1), d), jnp.where(own, devices, me)
        result_copy(d, dst, slot, jnp.where(k >= last, 1, 0)).start()

    stat_row = (rows + 7) // 8 * 8
    deep = lax.broadcasted_iota(jnp.int32, (8, HEAD_DIM), 0)

    def put_stats(d, high, total):
        block = jnp.zeros((8, HEAD_DIM), jnp.float32)
        for n, line in enumerate((high, total)):
            for m in range(3):
                part = line.astype(jnp.bfloat16).astype(jnp.float32)
                block = jnp.where(deep == 3 * n + m, part, block)
                line = line - part
        send_msg[d, stat_row : stat_row + 8, :] = block.astype(jnp.bfloat16)

    def message(ref, slot):
        block = ref[slot, stat_row : stat_row + 8, :].astype(jnp.float32)
        high = block[0:1] + block[1:2] + block[2:3]
        total = block[3:4] + block[4:5] + block[5:6]
        return high, total, ref[slot, 0:rows, :]

    def scores(g):
        gather(g)
        score = jnp.dot(
            q_heads[g].reshape(SEQS * QUERY_ROWS, HEAD_DIM), kt_buf[g], preferred_element_type=jnp.float32
        )
        score = score.reshape(SEQS, STEPS, PER_KV, tokens) + bias[...][:, None]
        score_buf[g % 2] = score
        return score.max(-1, keepdims=True)

    def finish(g, high):
        weight = jnp.exp2((score_buf[g % 2] - high) * EXP_SCALE)
        total = weight.sum(-1, keepdims=True)
        mixed = jnp.dot(
            weight.astype(jnp.bfloat16).reshape(SEQS * QUERY_ROWS, tokens),
            kv_buf[1, g],
            preferred_element_type=jnp.float32,
        )
        for s in range(SEQS):
            for t in range(STEPS):
                at = ((t * SEQS + s) * KV_HEADS + g) * PER_KV
                lo = (s * STEPS + t) * PER_KV
                part = mixed[lo : lo + PER_KV]
                if whole_groups:
                    d, off = at // rows, at % rows
                    send_msg[d, off : off + PER_KV, :] = part.astype(jnp.bfloat16)
                    spot = lane == sub + off
                    for which, column in enumerate((high, total)):
                        lines[d, which] = jnp.where(spot, column[s, t], lines.get((d, which), 0.0))
                    filled[d] += PER_KV
                    if filled[d] == rows:
                        ready.append(d)
                        put_stats(d, *(lines[d, n].sum(0, keepdims=True) for n in range(2)))
                else:
                    acc[at : at + PER_KV, :] = part
                    top[at : at + PER_KV, :] = jnp.broadcast_to(high[s, t], part.shape)
                    den[at : at + PER_KV, :] = jnp.broadcast_to(total[s, t], part.shape)

    sub = lax.broadcasted_iota(jnp.int32, (PER_KV, BLK), 0)
    lines, filled, ready = {}, [0] * devices, []
    ahead = scores(0)
    for g in range(KV_HEADS):
        high = ahead
        if g + 1 < KV_HEADS:
            ahead = scores(g + 1)
        finish(g, high)
        for d in sorted(ready) if early and g in SENDS else ():
            send_to(d)
            ready.remove(d)

    if not whole_groups:
        for d in range(devices):
            part = slice(d * rows, (d + 1) * rows)
            send_msg[d, 0:rows, :] = acc[part, :].astype(jnp.bfloat16)
            put_stats(d, as_row(top[part, :]), as_row(den[part, :]))
    if not early:
        for k in far:
            result_copy(target(k), target(k), me, int(k >= last)).start()

    def merge(parts):
        high = functools.reduce(jnp.maximum, [top for top, _, _ in parts])
        scales = [jnp.exp2((top - high) * EXP_SCALE) for top, _, _ in parts]
        total = functools.reduce(jnp.add, [a * den for a, (_, den, _) in zip(scales, parts)])
        return high, scales, total

    def weighted(scales, parts):
        terms = [as_column(a) * num.astype(jnp.float32) for a, (_, _, num) in zip(scales, parts)]
        return functools.reduce(jnp.add, terms)

    all_queries.wait_send()
    spare = 1 if early else 0
    together(recv_msg, last - 1 + spare, r_send.at[0], r_recv.at[0]).wait_recv()
    parts = [
        (own_stat[0:1, :], own_stat[1:2, :], own_num[...]),
        message(send_msg, me),
    ] + [message(recv_msg, source(k)) for k in range(1, last)]
    high, scales, total = merge(parts)
    parts = [(high, total, weighted(scales, parts))]
    together(send_msg, devices - 1 + spare, r_send.at[0], r_recv.at[0]).wait_send()
    together(recv_msg, devices - last, r_send.at[0], r_recv.at[1]).wait_recv()
    parts += [message(recv_msg, source(k)) for k in range(last, devices)]
    high, scales, total = merge(parts)
    total = jnp.where(total > 0.0, total, 1.0)
    result = weighted([a / total for a in scales], parts)
    out_ref[...] = result.astype(out_ref.dtype)


def shards(queries, new_kv, cache_keys, cache_values, context_lengths, block_table):
    devices = lax.axis_size("inner")
    rows = queries.shape[0]
    every = rows * devices
    deep = ((rows + 7) // 8 * 8 + 8 + 15) // 16 * 16
    tokens, width = cache_keys.shape
    dma = pltpu.SemaphoreType.DMA
    f32, bf16 = jnp.float32, jnp.bfloat16
    call = pl.pallas_call(
        functools.partial(kernel, devices),
        out_shape=jax.ShapeDtypeStruct(queries.shape, queries.dtype),
        in_specs=[pl.BlockSpec(memory_space=pltpu.HBM)] * 6,
        out_specs=pl.BlockSpec(memory_space=pltpu.VMEM),
        scratch_shapes=[
            pltpu.VMEM((2, KV_HEADS, tokens, HEAD_DIM), bf16),
            pltpu.VMEM((KV_HEADS, HEAD_DIM, tokens), bf16),
            pltpu.VMEM(new_kv.shape, bf16),
            pltpu.SMEM(context_lengths.shape, jnp.int32),
            pltpu.SMEM(block_table.shape, jnp.int32),
            pltpu.VMEM((rows, HEAD_DIM), bf16),
            pltpu.VMEM((devices, rows, HEAD_DIM), bf16),
            pltpu.VMEM((every, HEAD_DIM), f32),
            pltpu.VMEM((KV_HEADS, SEQS * STEPS, PER_KV, HEAD_DIM), bf16),
            pltpu.VMEM((SEQS, PER_KV, tokens), f32),
            pltpu.VMEM((PAIRS, width), f32),
            pltpu.VMEM((PAIRS, width), f32),
            pltpu.VMEM((rows, HEAD_DIM), f32),
            pltpu.VMEM((2, HEAD_DIM), f32),
            pltpu.VMEM((2, SEQS, STEPS, PER_KV, tokens), f32),
            pltpu.VMEM((every, HEAD_DIM), f32),
            pltpu.VMEM((every, HEAD_DIM), f32),
            pltpu.VMEM((every, HEAD_DIM), f32),
            pltpu.VMEM((devices, deep, HEAD_DIM), bf16),
            pltpu.VMEM((devices + 1, deep, HEAD_DIM), bf16),
            dma((5,)),
            dma((1,)),
            dma((1,)),
            dma((1,)),
            dma((2,)),
        ],
        compiler_params=pltpu.CompilerParams(
            collective_id=0, has_side_effects=True, vmem_limit_bytes=32 * 1024 * 1024
        ),
        name="paged_decode",
    )
    operands = (queries, new_kv, cache_keys, cache_values, context_lengths, block_table)
    return call(*(pltpu.with_memory_space_constraint(x, pltpu.HBM) for x in operands))


def solution(mesh):
    in_specs = (
        P(("parts", "inner"), None),
        P(None, None, "parts", None),
        P(("parts", "inner"), None),
        P(("parts", "inner"), None),
        P("parts"),
        P(("parts", "inner")),
    )
    out_specs = P(("parts", "inner"), None)
    return jax.shard_map(shards, mesh=mesh, in_specs=in_specs, out_specs=out_specs, check_vma=False)
```

```python
import functools
import math

import jax
import jax.numpy as jnp
from jax import lax
from jax.experimental import pallas as pl
from jax.experimental.pallas import tpu as pltpu
from jax.sharding import PartitionSpec as P

HEADS = 64
KV_HEADS = 8
HEAD_DIM = 128
SEQS = 2
BLK_DEV = 16
BLK = 128
STEPS = 3
PER_KV = HEADS // KV_HEADS
QUERY_ROWS = STEPS * PER_KV
PAIRS = 8
LOW = -1e30
EXP_SCALE = math.log2(math.e) / HEAD_DIM**0.5
MESH = pl.DeviceIdType.MESH
NT = (((1,), (1,)), ((), ()))


def kernel(
    devices,
    q_hbm, new_hbm, k_hbm, v_hbm, ctx_hbm, table_hbm,
    out_ref,
    kv_buf, kt_buf, new_buf, ctx_buf, table_buf,
    q_own, q_slots, q_flat, q_heads, bias,
    new_k, new_v, own_num, own_stat,
    score_buf, acc, top, den,
    send_msg, recv_msg,
    load_sem, q_send, q_recv, r_send, r_recv,
):
    me = lax.axis_index("inner")
    rows = q_hbm.shape[0]
    tokens = k_hbm.shape[0]
    max_blocks = 3 * BLK_DEV * devices // (2 * SEQS)

    power = devices & (devices - 1) == 0
    flips, bit = [], 1
    while bit < devices:
        flips.append((bit, bit * (1 - 2 * (me // bit % 2))))
        bit *= 2

    def target(k):
        if power:
            return me + sum(move for bit, move in flips if k & bit)
        return lax.rem(me + k, devices)

    def source(k):
        return target(k) if power else lax.rem(me + devices - k, devices)

    near = range(1, devices)
    far = range(devices - 1, 0, -1)
    load_q = pltpu.make_async_copy(q_hbm, q_own, load_sem.at[0])
    load_q.start()
    barrier = pltpu.get_barrier_semaphore()
    for k in far:
        pl.semaphore_signal(barrier, inc=1, device_id={"inner": target(k)}, device_id_type=MESH)

    small = (
        pltpu.make_async_copy(new_hbm, new_buf, load_sem.at[1]),
        pltpu.make_async_copy(ctx_hbm, ctx_buf, load_sem.at[2]),
        pltpu.make_async_copy(table_hbm, table_buf, load_sem.at[3]),
    )
    for copy in small:
        copy.start()
    loads = []
    for n, src in enumerate((k_hbm, v_hbm)):
        for g in range(KV_HEADS):
            part = pl.ds(g * HEAD_DIM, HEAD_DIM)
            loads.append(pltpu.make_async_copy(src.at[:, part], kv_buf.at[n, g], load_sem.at[4]))
    for copy in loads:
        copy.start()

    def query_copy(k, slot):
        return pltpu.make_async_remote_copy(
            src_ref=q_own,
            dst_ref=q_slots.at[slot],
            send_sem=q_send.at[0],
            recv_sem=q_recv.at[0],
            device_id={"inner": target(k)},
            device_id_type=MESH,
        )

    load_q.wait()
    pl.semaphore_wait(barrier, devices - 1)
    for k in far:
        query_copy(k, me).start()
    q_slots[me] = q_own[...]
    for copy in small:
        copy.wait()

    lane = lax.broadcasted_iota(jnp.int32, (8, BLK), 1)
    for b in range(tokens // BLK):
        entry = table_buf[b]
        owner = jnp.where(entry >= 0, entry // max_blocks, -1)
        first = jnp.where(entry >= 0, entry % max_blocks, 0) * BLK
        for s in range(SEQS):
            count = jnp.where(owner == s, ctx_buf[s] - first, 0)
            bias[s, :, b * BLK : (b + 1) * BLK] = jnp.where(lane < count, 0.0, LOW)

    new_k[...] = jnp.zeros_like(new_k)
    new_v[...] = jnp.zeros_like(new_v)
    for u in range(STEPS):
        new_k[u * SEQS : (u + 1) * SEQS, :] = new_buf[0, u].astype(jnp.float32)
        new_v[u * SEQS : (u + 1) * SEQS, :] = new_buf[1, u].astype(jnp.float32)

    def stacked(ref):
        parts = [ref[:, g * HEAD_DIM : (g + 1) * HEAD_DIM] for g in range(KV_HEADS)]
        return jnp.concatenate(parts, axis=0).astype(jnp.bfloat16)

    own_q = q_own[...]
    score = lax.dot_general(own_q, stacked(new_k), NT, preferred_element_type=jnp.float32)
    row = me * rows + lax.broadcasted_iota(jnp.int32, score.shape, 0)
    col = lax.broadcasted_iota(jnp.int32, score.shape, 1)
    pair = col % PAIRS
    allowed = (
        (pair < STEPS * SEQS)
        & (col // PAIRS == row % HEADS // PER_KV)
        & (pair % SEQS == row // HEADS % SEQS)
        & (pair // SEQS <= row // (HEADS * SEQS))
    )
    score = jnp.where(allowed, score, LOW)
    own_top = score.max(-1, keepdims=True)
    weight = jnp.where(allowed, jnp.exp2((score - own_top) * EXP_SCALE), 0.0)
    own_den = weight.sum(-1, keepdims=True)
    own_num[...] = jnp.dot(
        weight.astype(jnp.bfloat16), stacked(new_v), preferred_element_type=jnp.float32
    )
    eye = lax.broadcasted_iota(jnp.int32, (rows, HEAD_DIM), 0) == lax.broadcasted_iota(
        jnp.int32, (rows, HEAD_DIM), 1
    )

    def as_row(column):
        return jnp.sum(jnp.where(eye, column, 0.0), axis=0, keepdims=True)

    def as_column(line):
        return jnp.sum(jnp.where(eye, line, 0.0), axis=1, keepdims=True)

    own_stat[0:1, :] = as_row(own_top)
    own_stat[1:2, :] = as_row(own_den)

    def together(ref, count, out_sem, in_sem):
        part = ref.at[pl.ds(0, count)]
        return pltpu.make_async_remote_copy(
            src_ref=part,
            dst_ref=part,
            send_sem=out_sem,
            recv_sem=in_sem,
            device_id={"inner": target(1)},
            device_id_type=MESH,
        )

    pltpu.make_async_copy(kv_buf, kv_buf, load_sem.at[4]).wait()
    for g in range(KV_HEADS):
        kt_buf[g] = kv_buf[0, g].T
    all_queries = together(q_slots, devices - 1, q_send.at[0], q_recv.at[0])
    all_queries.wait_recv()

    whole_groups = rows % PER_KV == 0
    early = power and whole_groups
    if not whole_groups:
        for d in range(devices):
            q_flat[d * rows : (d + 1) * rows, :] = q_slots[d].astype(jnp.float32)

    def gather(g):
        for s in range(SEQS):
            for t in range(STEPS):
                at = ((t * SEQS + s) * KV_HEADS + g) * PER_KV
                if whole_groups:
                    d, off = at // rows, at % rows
                    q_heads[g, s * STEPS + t] = q_slots[d, off : off + PER_KV, :]
                else:
                    q_heads[g, s * STEPS + t] = q_flat[at : at + PER_KV, :].astype(jnp.bfloat16)

    last = devices - devices // 4

    def result_copy(src, dst, slot, late):
        return pltpu.make_async_remote_copy(
            src_ref=send_msg.at[src],
            dst_ref=recv_msg.at[slot],
            send_sem=r_send.at[0],
            recv_sem=r_recv.at[late],
            device_id={"inner": dst},
            device_id_type=MESH,
        )

    def send_to(d):
        k = 0
        for bit, move in flips:
            here = me // bit % 2
            k = k + bit * (1 - here if d & bit else here)
        own = me == d
        dst, slot = jnp.where(own, target(1), d), jnp.where(own, devices, me)
        result_copy(d, dst, slot, jnp.where(k >= last, 1, 0)).start()

    stat_row = (rows + 7) // 8 * 8
    deep = lax.broadcasted_iota(jnp.int32, (8, HEAD_DIM), 0)

    def put_stats(d, high, total):
        block = jnp.zeros((8, HEAD_DIM), jnp.float32)
        for n, line in enumerate((high, total)):
            for m in range(3):
                part = line.astype(jnp.bfloat16).astype(jnp.float32)
                block = jnp.where(deep == 3 * n + m, part, block)
                line = line - part
        send_msg[d, stat_row : stat_row + 8, :] = block.astype(jnp.bfloat16)

    def message(ref, slot):
        block = ref[slot, stat_row : stat_row + 8, :].astype(jnp.float32)
        high = block[0:1] + block[1:2] + block[2:3]
        total = block[3:4] + block[4:5] + block[5:6]
        return high, total, ref[slot, 0:rows, :]

    def scores(g):
        gather(g)
        score = jnp.dot(
            q_heads[g].reshape(SEQS * QUERY_ROWS, HEAD_DIM), kt_buf[g], preferred_element_type=jnp.float32
        )
        score = score.reshape(SEQS, STEPS, PER_KV, tokens) + bias[...][:, None]
        score_buf[g] = score
        return score.max(-1, keepdims=True)

    def finish(g, high):
        weight = jnp.exp2((score_buf[g] - high) * EXP_SCALE)
        total = weight.sum(-1, keepdims=True)
        mixed = jnp.dot(
            weight.astype(jnp.bfloat16).reshape(SEQS * QUERY_ROWS, tokens),
            kv_buf[1, g],
            preferred_element_type=jnp.float32,
        )
        for s in range(SEQS):
            for t in range(STEPS):
                at = ((t * SEQS + s) * KV_HEADS + g) * PER_KV
                lo = (s * STEPS + t) * PER_KV
                part = mixed[lo : lo + PER_KV]
                if whole_groups:
                    d, off = at // rows, at % rows
                    send_msg[d, off : off + PER_KV, :] = part.astype(jnp.bfloat16)
                    spot = lane == sub + off
                    for which, column in enumerate((high, total)):
                        lines[d, which] = jnp.where(spot, column[s, t], lines.get((d, which), 0.0))
                    filled[d] += PER_KV
                    if filled[d] == rows:
                        ready.append(d)
                        put_stats(d, *(lines[d, n].sum(0, keepdims=True) for n in range(2)))
                else:
                    acc[at : at + PER_KV, :] = part
                    top[at : at + PER_KV, :] = jnp.broadcast_to(high[s, t], part.shape)
                    den[at : at + PER_KV, :] = jnp.broadcast_to(total[s, t], part.shape)

    sub = lax.broadcasted_iota(jnp.int32, (PER_KV, BLK), 0)
    lines, filled, ready = {}, [0] * devices, []
    highs = {g: scores(g) for g in range(4)}
    for group, after in (((0, 1, 2), (4, 5, 6)), ((3, 4, 5), (7,)), ((6, 7), ())):
        for g in group:
            finish(g, highs[g])
        if early:
            for d in sorted(ready) if early else ():
                send_to(d)
                ready.remove(d)
        for g in after:
            highs[g] = scores(g)
    if not whole_groups:
        for d in range(devices):
            part = slice(d * rows, (d + 1) * rows)
            send_msg[d, 0:rows, :] = acc[part, :].astype(jnp.bfloat16)
            put_stats(d, as_row(top[part, :]), as_row(den[part, :]))
    if not early:
        for k in far:
            result_copy(target(k), target(k), me, int(k >= last)).start()

    def merge(parts):
        high = functools.reduce(jnp.maximum, [top for top, _, _ in parts])
        scales = [jnp.exp2((top - high) * EXP_SCALE) for top, _, _ in parts]
        total = functools.reduce(jnp.add, [a * den for a, (_, den, _) in zip(scales, parts)])
        return high, scales, total

    def weighted(scales, parts):
        terms = [as_column(a) * num.astype(jnp.float32) for a, (_, _, num) in zip(scales, parts)]
        return functools.reduce(jnp.add, terms)

    all_queries.wait_send()
    spare = 1 if early else 0
    together(recv_msg, last - 1 + spare, r_send.at[0], r_recv.at[0]).wait_recv()
    parts = [
        (own_stat[0:1, :], own_stat[1:2, :], own_num[...]),
        message(send_msg, me),
    ] + [message(recv_msg, source(k)) for k in range(1, last)]
    high, scales, total = merge(parts)
    parts = [(high, total, weighted(scales, parts))]
    together(send_msg, devices - 1 + spare, r_send.at[0], r_recv.at[0]).wait_send()
    together(recv_msg, devices - last, r_send.at[0], r_recv.at[1]).wait_recv()
    parts += [message(recv_msg, source(k)) for k in range(last, devices)]
    high, scales, total = merge(parts)
    total = jnp.where(total > 0.0, total, 1.0)
    result = weighted([a / total for a in scales], parts)
    out_ref[...] = result.astype(out_ref.dtype)


def shards(queries, new_kv, cache_keys, cache_values, context_lengths, block_table):
    devices = lax.axis_size("inner")
    rows = queries.shape[0]
    every = rows * devices
    deep = ((rows + 7) // 8 * 8 + 8 + 15) // 16 * 16
    tokens, width = cache_keys.shape
    dma = pltpu.SemaphoreType.DMA
    f32, bf16 = jnp.float32, jnp.bfloat16
    call = pl.pallas_call(
        functools.partial(kernel, devices),
        out_shape=jax.ShapeDtypeStruct(queries.shape, queries.dtype),
        in_specs=[pl.BlockSpec(memory_space=pltpu.HBM)] * 6,
        out_specs=pl.BlockSpec(memory_space=pltpu.VMEM),
        scratch_shapes=[
            pltpu.VMEM((2, KV_HEADS, tokens, HEAD_DIM), bf16),
            pltpu.VMEM((KV_HEADS, HEAD_DIM, tokens), bf16),
            pltpu.VMEM(new_kv.shape, bf16),
            pltpu.SMEM(context_lengths.shape, jnp.int32),
            pltpu.SMEM(block_table.shape, jnp.int32),
            pltpu.VMEM((rows, HEAD_DIM), bf16),
            pltpu.VMEM((devices, rows, HEAD_DIM), bf16),
            pltpu.VMEM((every, HEAD_DIM), f32),
            pltpu.VMEM((KV_HEADS, SEQS * STEPS, PER_KV, HEAD_DIM), bf16),
            pltpu.VMEM((SEQS, PER_KV, tokens), f32),
            pltpu.VMEM((PAIRS, width), f32),
            pltpu.VMEM((PAIRS, width), f32),
            pltpu.VMEM((rows, HEAD_DIM), f32),
            pltpu.VMEM((2, HEAD_DIM), f32),
            pltpu.VMEM((KV_HEADS, SEQS, STEPS, PER_KV, tokens), f32),
            pltpu.VMEM((every, HEAD_DIM), f32),
            pltpu.VMEM((every, HEAD_DIM), f32),
            pltpu.VMEM((every, HEAD_DIM), f32),
            pltpu.VMEM((devices, deep, HEAD_DIM), bf16),
            pltpu.VMEM((devices + 1, deep, HEAD_DIM), bf16),
            dma((5,)),
            dma((1,)),
            dma((1,)),
            dma((1,)),
            dma((2,)),
        ],
        compiler_params=pltpu.CompilerParams(
            collective_id=0, has_side_effects=True, vmem_limit_bytes=32 * 1024 * 1024
        ),
        name="paged_decode",
    )
    operands = (queries, new_kv, cache_keys, cache_values, context_lengths, block_table)
    return call(*(pltpu.with_memory_space_constraint(x, pltpu.HBM) for x in operands))


def solution(mesh):
    in_specs = (
        P(("parts", "inner"), None),
        P(None, None, "parts", None),
        P(("parts", "inner"), None),
        P(("parts", "inner"), None),
        P("parts"),
        P(("parts", "inner")),
    )
    out_specs = P(("parts", "inner"), None)
    return jax.shard_map(shards, mesh=mesh, in_specs=in_specs, out_specs=out_specs, check_vma=False)
```

```python
import functools
import math

import jax
import jax.numpy as jnp
from jax import lax
from jax.experimental import pallas as pl
from jax.experimental.pallas import tpu as pltpu
from jax.sharding import PartitionSpec as P

HEADS = 64
KV_HEADS = 8
HEAD_DIM = 128
SEQS = 2
BLK_DEV = 16
BLK = 128
STEPS = 3
PER_KV = HEADS // KV_HEADS
QUERY_ROWS = STEPS * PER_KV
PAIRS = 8
LOW = -1e30
EXP_SCALE = math.log2(math.e) / HEAD_DIM**0.5
MESH = pl.DeviceIdType.MESH
NT = (((1,), (1,)), ((), ()))


def kernel(
    devices,
    q_hbm, new_hbm, k_hbm, v_hbm, ctx_hbm, table_hbm,
    out_ref,
    kv_buf, kt_buf, new_buf, ctx_buf, table_buf,
    q_own, q_slots, q_flat, q_heads, bias,
    new_k, new_v, own_num, own_stat,
    score_buf, acc, top, den,
    send_msg, recv_msg,
    load_sem, q_send, q_recv, r_send, r_recv,
):
    me = lax.axis_index("inner")
    rows = q_hbm.shape[0]
    tokens = k_hbm.shape[0]
    max_blocks = 3 * BLK_DEV * devices // (2 * SEQS)

    power = devices & (devices - 1) == 0
    flips, bit = [], 1
    while bit < devices:
        flips.append((bit, bit * (1 - 2 * (me // bit % 2))))
        bit *= 2

    def target(k):
        if power:
            return me + sum(move for bit, move in flips if k & bit)
        return lax.rem(me + k, devices)

    def source(k):
        return target(k) if power else lax.rem(me + devices - k, devices)

    near = range(1, devices)
    far = range(devices - 1, 0, -1)
    load_q = pltpu.make_async_copy(q_hbm, q_own, load_sem.at[0])
    load_q.start()
    whole_groups = rows % PER_KV == 0
    early = power and whole_groups
    relay = early and devices >= 16
    quarter = devices // 4
    plane, column = me // quarter, me % quarter
    hub = plane == 1

    def place(d):
        return d % quarter * 4 + d // quarter if relay else d

    mine = place(me)
    barrier = pltpu.get_barrier_semaphore()

    def signal(semaphore, d):
        pl.semaphore_signal(semaphore, inc=1, device_id={"inner": d}, device_id_type=MESH)

    if relay:
        for d in [*range(quarter, 2 * quarter), *range(devices - 1, 2 * quarter - 1, -1), *range(quarter)]:
            pl.when(me != d if d >= quarter else me == d + quarter)(functools.partial(signal, barrier, d))
    else:
        for k in far:
            signal(barrier, target(k))

    small = (
        pltpu.make_async_copy(new_hbm, new_buf, load_sem.at[1]),
        pltpu.make_async_copy(ctx_hbm, ctx_buf, load_sem.at[2]),
        pltpu.make_async_copy(table_hbm, table_buf, load_sem.at[3]),
    )
    for copy in small:
        copy.start()
    loads = []
    for n, src in enumerate((k_hbm, v_hbm)):
        for g in range(KV_HEADS):
            part = pl.ds(g * HEAD_DIM, HEAD_DIM)
            loads.append(pltpu.make_async_copy(src.at[:, part], kv_buf.at[n, g], load_sem.at[4]))
    for copy in loads:
        copy.start()

    def query_copy(d, into):
        return pltpu.make_async_remote_copy(
            src_ref=q_own,
            dst_ref=q_slots.at[mine],
            send_sem=q_send.at[0],
            recv_sem=q_recv.at[into],
            device_id={"inner": d},
            device_id_type=MESH,
        )

    def pair_copy(d, out):
        pair = q_slots.at[pl.ds(column * 4, 2)]
        return pltpu.make_async_remote_copy(
            src_ref=pair,
            dst_ref=pair,
            send_sem=q_send.at[out],
            recv_sem=q_recv.at[0],
            device_id={"inner": d},
            device_id_type=MESH,
        )

    def others():
        return [(column + n) % quarter for n in range(1, quarter)]

    def together(ref, count, out_sem, in_sem):
        part = ref.at[pl.ds(0, count)]
        return pltpu.make_async_remote_copy(
            src_ref=part,
            dst_ref=part,
            send_sem=out_sem,
            recv_sem=in_sem,
            device_id={"inner": target(1)},
            device_id_type=MESH,
        )

    load_q.wait()
    q_slots[mine] = q_own[...]
    if relay:
        pl.semaphore_wait(barrier, jnp.where(plane == 0, 1, devices - 1))

        even = pltpu.make_async_copy(q_own, q_slots.at[devices], q_recv.at[jnp.where(hub, 0, 1)])
        even.start()

        @pl.when(plane == 0)
        def _():
            query_copy(me + quarter, 1).start()

        together(q_slots, 1, q_send.at[0], q_recv.at[1]).wait_recv()

        @pl.when(hub)
        def _():
            for d in [*range(3 * quarter, devices), *range(2 * quarter, 3 * quarter)]:
                pair_copy(d, 1).start()
            for d in others():
                pair_copy(quarter + d, 2).start()
            for d in others():
                pair_copy(d, 2).start()
            query_copy(column, 0).start()

        @pl.when(plane > 1)
        def _():
            for k in far:
                query_copy(target(k), 0).start()
    else:
        pl.semaphore_wait(barrier, devices - 1)
        for k in far:
            query_copy(target(k), 0).start()
    for copy in small:
        copy.wait()

    lane = lax.broadcasted_iota(jnp.int32, (8, BLK), 1)
    for b in range(tokens // BLK):
        entry = table_buf[b]
        owner = jnp.where(entry >= 0, entry // max_blocks, -1)
        first = jnp.where(entry >= 0, entry % max_blocks, 0) * BLK
        for s in range(SEQS):
            count = jnp.where(owner == s, ctx_buf[s] - first, 0)
            bias[s, :, b * BLK : (b + 1) * BLK] = jnp.where(lane < count, 0.0, LOW)

    new_k[...] = jnp.zeros_like(new_k)
    new_v[...] = jnp.zeros_like(new_v)
    for u in range(STEPS):
        new_k[u * SEQS : (u + 1) * SEQS, :] = new_buf[0, u].astype(jnp.float32)
        new_v[u * SEQS : (u + 1) * SEQS, :] = new_buf[1, u].astype(jnp.float32)

    def stacked(ref):
        parts = [ref[:, g * HEAD_DIM : (g + 1) * HEAD_DIM] for g in range(KV_HEADS)]
        return jnp.concatenate(parts, axis=0).astype(jnp.bfloat16)

    own_q = q_own[...]
    score = lax.dot_general(own_q, stacked(new_k), NT, preferred_element_type=jnp.float32)
    row = me * rows + lax.broadcasted_iota(jnp.int32, score.shape, 0)
    col = lax.broadcasted_iota(jnp.int32, score.shape, 1)
    pair = col % PAIRS
    allowed = (
        (pair < STEPS * SEQS)
        & (col // PAIRS == row % HEADS // PER_KV)
        & (pair % SEQS == row // HEADS % SEQS)
        & (pair // SEQS <= row // (HEADS * SEQS))
    )
    score = jnp.where(allowed, score, LOW)
    own_top = score.max(-1, keepdims=True)
    weight = jnp.where(allowed, jnp.exp2((score - own_top) * EXP_SCALE), 0.0)
    own_den = weight.sum(-1, keepdims=True)
    own_num[...] = jnp.dot(
        weight.astype(jnp.bfloat16), stacked(new_v), preferred_element_type=jnp.float32
    )
    eye = lax.broadcasted_iota(jnp.int32, (rows, HEAD_DIM), 0) == lax.broadcasted_iota(
        jnp.int32, (rows, HEAD_DIM), 1
    )

    def as_row(column):
        return jnp.sum(jnp.where(eye, column, 0.0), axis=0, keepdims=True)

    def as_column(line):
        return jnp.sum(jnp.where(eye, line, 0.0), axis=1, keepdims=True)

    own_stat[0:1, :] = as_row(own_top)
    own_stat[1:2, :] = as_row(own_den)

    pltpu.make_async_copy(kv_buf, kv_buf, load_sem.at[4]).wait()
    def sent(count, n):
        together(q_slots, count, q_send.at[n], q_recv.at[0]).wait_send()

    if relay:
        pl.when(plane <= 1)(functools.partial(sent, 1, 0))
        for n, count in ((1, 4 * quarter), (2, 4 * quarter - 4)):
            pl.when(hub)(functools.partial(sent, count, n))
        pl.when(plane > 1)(functools.partial(sent, devices - 1, 0))
    else:
        sent(devices - 1, 0)
    for g in range(KV_HEADS):
        kt_buf[g] = kv_buf[0, g].T
    together(q_slots, devices - 1, q_send.at[0], q_recv.at[0]).wait_recv()

    if not whole_groups:
        for d in range(devices):
            q_flat[d * rows : (d + 1) * rows, :] = q_slots[d].astype(jnp.float32)

    def gather(g):
        for s in range(SEQS):
            for t in range(STEPS):
                at = ((t * SEQS + s) * KV_HEADS + g) * PER_KV
                if whole_groups:
                    d, off = at // rows, at % rows
                    q_heads[g, s * STEPS + t] = q_slots[place(d), off : off + PER_KV, :]
                else:
                    q_heads[g, s * STEPS + t] = q_flat[at : at + PER_KV, :].astype(jnp.bfloat16)

    last = devices - devices // 4

    def result_copy(src, dst, slot, late):
        return pltpu.make_async_remote_copy(
            src_ref=send_msg.at[src],
            dst_ref=recv_msg.at[slot],
            send_sem=r_send.at[0],
            recv_sem=r_recv.at[late],
            device_id={"inner": dst},
            device_id_type=MESH,
        )

    def send_to(d):
        k = 0
        for bit, move in flips:
            here = me // bit % 2
            k = k + bit * (1 - here if d & bit else here)
        own = me == d
        dst, slot = jnp.where(own, target(1), d), jnp.where(own, devices, me)
        result_copy(d, dst, slot, jnp.where(k >= last, 1, 0)).start()

    stat_row = (rows + 7) // 8 * 8
    deep = lax.broadcasted_iota(jnp.int32, (8, HEAD_DIM), 0)

    def put_stats(d, high, total):
        block = jnp.zeros((8, HEAD_DIM), jnp.float32)
        for n, line in enumerate((high, total)):
            for m in range(3):
                part = line.astype(jnp.bfloat16).astype(jnp.float32)
                block = jnp.where(deep == 3 * n + m, part, block)
                line = line - part
        send_msg[d, stat_row : stat_row + 8, :] = block.astype(jnp.bfloat16)

    def message(ref, slot):
        block = ref[slot, stat_row : stat_row + 8, :].astype(jnp.float32)
        high = block[0:1] + block[1:2] + block[2:3]
        total = block[3:4] + block[4:5] + block[5:6]
        return high, total, ref[slot, 0:rows, :]

    def scores(g):
        gather(g)
        score = jnp.dot(
            q_heads[g].reshape(SEQS * QUERY_ROWS, HEAD_DIM), kt_buf[g], preferred_element_type=jnp.float32
        )
        score = score.reshape(SEQS, STEPS, PER_KV, tokens) + bias[...][:, None]
        score_buf[g] = score
        return score.max(-1, keepdims=True)

    def finish(g, high):
        weight = jnp.exp2((score_buf[g] - high) * EXP_SCALE)
        total = weight.sum(-1, keepdims=True)
        mixed = jnp.dot(
            weight.astype(jnp.bfloat16).reshape(SEQS * QUERY_ROWS, tokens),
            kv_buf[1, g],
            preferred_element_type=jnp.float32,
        )
        for s in range(SEQS):
            for t in range(STEPS):
                at = ((t * SEQS + s) * KV_HEADS + g) * PER_KV
                lo = (s * STEPS + t) * PER_KV
                part = mixed[lo : lo + PER_KV]
                if whole_groups:
                    d, off = at // rows, at % rows
                    send_msg[d, off : off + PER_KV, :] = part.astype(jnp.bfloat16)
                    spot = lane == sub + off
                    for which, column in enumerate((high, total)):
                        lines[d, which] = jnp.where(spot, column[s, t], lines.get((d, which), 0.0))
                    filled[d] += PER_KV
                    if filled[d] == rows:
                        ready.append(d)
                        put_stats(d, *(lines[d, n].sum(0, keepdims=True) for n in range(2)))
                else:
                    acc[at : at + PER_KV, :] = part
                    top[at : at + PER_KV, :] = jnp.broadcast_to(high[s, t], part.shape)
                    den[at : at + PER_KV, :] = jnp.broadcast_to(total[s, t], part.shape)

    sub = lax.broadcasted_iota(jnp.int32, (PER_KV, BLK), 0)
    lines, filled, ready = {}, [0] * devices, []
    highs = {g: scores(g) for g in range(4)}
    for group, after in (((0, 1, 2), (4, 5, 6)), ((3, 4, 5), (7,)), ((6, 7), ())):
        for g in group:
            finish(g, highs[g])
        if early:
            for d in sorted(ready) if early else ():
                send_to(d)
                ready.remove(d)
        for g in after:
            highs[g] = scores(g)
    if not whole_groups:
        for d in range(devices):
            part = slice(d * rows, (d + 1) * rows)
            send_msg[d, 0:rows, :] = acc[part, :].astype(jnp.bfloat16)
            put_stats(d, as_row(top[part, :]), as_row(den[part, :]))
    if not early:
        for k in far:
            result_copy(target(k), target(k), me, int(k >= last)).start()

    def merge(parts):
        high = functools.reduce(jnp.maximum, [top for top, _, _ in parts])
        scales = [jnp.exp2((top - high) * EXP_SCALE) for top, _, _ in parts]
        total = functools.reduce(jnp.add, [a * den for a, (_, den, _) in zip(scales, parts)])
        return high, scales, total

    def weighted(scales, parts):
        terms = [as_column(a) * num.astype(jnp.float32) for a, (_, _, num) in zip(scales, parts)]
        return functools.reduce(jnp.add, terms)

    spare = 1 if early else 0
    together(recv_msg, last - 1 + spare, r_send.at[0], r_recv.at[0]).wait_recv()
    parts = [
        (own_stat[0:1, :], own_stat[1:2, :], own_num[...]),
        message(send_msg, me),
    ] + [message(recv_msg, source(k)) for k in range(1, last)]
    high, scales, total = merge(parts)
    parts = [(high, total, weighted(scales, parts))]
    together(send_msg, devices - 1 + spare, r_send.at[0], r_recv.at[0]).wait_send()
    together(recv_msg, devices - last, r_send.at[0], r_recv.at[1]).wait_recv()
    parts += [message(recv_msg, source(k)) for k in range(last, devices)]
    high, scales, total = merge(parts)
    total = jnp.where(total > 0.0, total, 1.0)
    result = weighted([a / total for a in scales], parts)
    out_ref[...] = result.astype(out_ref.dtype)


def shards(queries, new_kv, cache_keys, cache_values, context_lengths, block_table):
    devices = lax.axis_size("inner")
    rows = queries.shape[0]
    every = rows * devices
    deep = ((rows + 7) // 8 * 8 + 8 + 15) // 16 * 16
    tokens, width = cache_keys.shape
    dma = pltpu.SemaphoreType.DMA
    f32, bf16 = jnp.float32, jnp.bfloat16
    call = pl.pallas_call(
        functools.partial(kernel, devices),
        out_shape=jax.ShapeDtypeStruct(queries.shape, queries.dtype),
        in_specs=[pl.BlockSpec(memory_space=pltpu.HBM)] * 6,
        out_specs=pl.BlockSpec(memory_space=pltpu.VMEM),
        scratch_shapes=[
            pltpu.VMEM((2, KV_HEADS, tokens, HEAD_DIM), bf16),
            pltpu.VMEM((KV_HEADS, HEAD_DIM, tokens), bf16),
            pltpu.VMEM(new_kv.shape, bf16),
            pltpu.SMEM(context_lengths.shape, jnp.int32),
            pltpu.SMEM(block_table.shape, jnp.int32),
            pltpu.VMEM((rows, HEAD_DIM), bf16),
            pltpu.VMEM((devices + 1, rows, HEAD_DIM), bf16),
            pltpu.VMEM((every, HEAD_DIM), f32),
            pltpu.VMEM((KV_HEADS, SEQS * STEPS, PER_KV, HEAD_DIM), bf16),
            pltpu.VMEM((SEQS, PER_KV, tokens), f32),
            pltpu.VMEM((PAIRS, width), f32),
            pltpu.VMEM((PAIRS, width), f32),
            pltpu.VMEM((rows, HEAD_DIM), f32),
            pltpu.VMEM((2, HEAD_DIM), f32),
            pltpu.VMEM((KV_HEADS, SEQS, STEPS, PER_KV, tokens), f32),
            pltpu.VMEM((every, HEAD_DIM), f32),
            pltpu.VMEM((every, HEAD_DIM), f32),
            pltpu.VMEM((every, HEAD_DIM), f32),
            pltpu.VMEM((devices, deep, HEAD_DIM), bf16),
            pltpu.VMEM((devices + 1, deep, HEAD_DIM), bf16),
            dma((5,)),
            dma((3,)),
            dma((2,)),
            dma((1,)),
            dma((2,)),
        ],
        compiler_params=pltpu.CompilerParams(
            collective_id=0, has_side_effects=True, vmem_limit_bytes=32 * 1024 * 1024
        ),
        name="paged_decode",
    )
    operands = (queries, new_kv, cache_keys, cache_values, context_lengths, block_table)
    return call(*(pltpu.with_memory_space_constraint(x, pltpu.HBM) for x in operands))


def solution(mesh):
    in_specs = (
        P(("parts", "inner"), None),
        P(None, None, "parts", None),
        P(("parts", "inner"), None),
        P(("parts", "inner"), None),
        P("parts"),
        P(("parts", "inner")),
    )
    out_specs = P(("parts", "inner"), None)
    return jax.shard_map(shards, mesh=mesh, in_specs=in_specs, out_specs=out_specs, check_vma=False)
```

```python
import functools
import math

import jax
import jax.numpy as jnp
from jax import lax
from jax.experimental import pallas as pl
from jax.experimental.pallas import tpu as pltpu
from jax.sharding import PartitionSpec as P

HEADS = 64
KV_HEADS = 8
HEAD_DIM = 128
SEQS = 2
BLK_DEV = 16
BLK = 128
STEPS = 3
PER_KV = HEADS // KV_HEADS
QUERY_ROWS = STEPS * PER_KV
PAIRS = 8
LOW = -1e30
EXP_SCALE = math.log2(math.e) / HEAD_DIM**0.5
MESH = pl.DeviceIdType.MESH
NT = (((1,), (1,)), ((), ()))


def kernel(
    devices,
    q_hbm, new_hbm, k_hbm, v_hbm, ctx_hbm, table_hbm,
    out_ref,
    kv_buf, kt_buf, new_buf, ctx_buf, table_buf,
    q_own, q_slots, q_flat, q_heads, bias,
    new_k, new_v, own_num, own_stat,
    score_buf, acc, top, den,
    send_msg, recv_msg,
    load_sem, q_send, q_recv, r_send, r_recv,
):
    me = lax.axis_index("inner")
    rows = q_hbm.shape[0]
    tokens = k_hbm.shape[0]
    max_blocks = 3 * BLK_DEV * devices // (2 * SEQS)

    power = devices & (devices - 1) == 0
    flips, bit = [], 1
    while bit < devices:
        flips.append((bit, bit * (1 - 2 * (me // bit % 2))))
        bit *= 2

    def target(k):
        if power:
            return me + sum(move for bit, move in flips if k & bit)
        return lax.rem(me + k, devices)

    def source(k):
        return target(k) if power else lax.rem(me + devices - k, devices)

    near = range(1, devices)
    far = range(devices - 1, 0, -1)
    load_q = pltpu.make_async_copy(q_hbm, q_own, q_send.at[0])
    load_q.start()
    small = (
        pltpu.make_async_copy(new_hbm, new_buf, q_send.at[1]),
        pltpu.make_async_copy(ctx_hbm, ctx_buf, q_send.at[2]),
        pltpu.make_async_copy(table_hbm, table_buf, r_send.at[0]),
    )
    for copy in small:
        copy.start()
    whole_groups = rows % PER_KV == 0
    early = power and whole_groups
    relay = early and devices >= 16
    quarter = devices // 4
    plane, column = me // quarter, me % quarter
    hub = plane == 1

    def place(d):
        return d % quarter * 4 + d // quarter if relay else d

    mine = place(me)
    barrier = pltpu.get_barrier_semaphore()

    def signal(semaphore, d):
        pl.semaphore_signal(semaphore, inc=1, device_id={"inner": d}, device_id_type=MESH)

    if relay:
        for d in [*range(quarter, 2 * quarter), *range(devices - 1, 2 * quarter - 1, -1), *range(quarter)]:
            pl.when(me != d if d >= quarter else me == d + quarter)(functools.partial(signal, barrier, d))
    else:
        for k in far:
            signal(barrier, target(k))

    loads = []
    for n, src in enumerate((k_hbm, v_hbm)):
        for g in range(KV_HEADS):
            part = pl.ds(g * HEAD_DIM, HEAD_DIM)
            loads.append(pltpu.make_async_copy(src.at[:, part], kv_buf.at[n, g], load_sem.at[0]))
    for copy in loads:
        copy.start()

    def query_copy(d, into):
        return pltpu.make_async_remote_copy(
            src_ref=q_own,
            dst_ref=q_slots.at[mine],
            send_sem=q_send.at[0],
            recv_sem=q_recv.at[into],
            device_id={"inner": d},
            device_id_type=MESH,
        )

    def pair_copy(d, out):
        pair = q_slots.at[pl.ds(column * 4, 2)]
        return pltpu.make_async_remote_copy(
            src_ref=pair,
            dst_ref=pair,
            send_sem=q_send.at[out],
            recv_sem=q_recv.at[0],
            device_id={"inner": d},
            device_id_type=MESH,
        )

    def others():
        return [(column + n) % quarter for n in range(1, quarter)]

    def together(ref, count, out_sem, in_sem):
        part = ref.at[pl.ds(0, count)]
        return pltpu.make_async_remote_copy(
            src_ref=part,
            dst_ref=part,
            send_sem=out_sem,
            recv_sem=in_sem,
            device_id={"inner": target(1)},
            device_id_type=MESH,
        )

    load_q.wait()
    for copy in small:
        copy.wait()
    q_slots[mine] = q_own[...]
    if relay:
        pl.semaphore_wait(barrier, jnp.where(plane == 0, 1, devices - 1))

        even = pltpu.make_async_copy(q_own, q_slots.at[devices], q_recv.at[jnp.where(hub, 0, 1)])
        even.start()

        @pl.when(plane == 0)
        def _():
            query_copy(me + quarter, 1).start()

        together(q_slots, 1, q_send.at[0], q_recv.at[1]).wait_recv()

        @pl.when(hub)
        def _():
            for d in [*range(3 * quarter, devices), *range(2 * quarter, 3 * quarter)]:
                pair_copy(d, 1).start()
            for d in others():
                pair_copy(quarter + d, 2).start()
            for d in others():
                pair_copy(d, 2).start()
            query_copy(column, 0).start()

        @pl.when(plane > 1)
        def _():
            for k in far:
                query_copy(target(k), 0).start()
    else:
        pl.semaphore_wait(barrier, devices - 1)
        for k in far:
            query_copy(target(k), 0).start()

    lane = lax.broadcasted_iota(jnp.int32, (8, BLK), 1)
    for b in range(tokens // BLK):
        entry = table_buf[b]
        owner = jnp.where(entry >= 0, entry // max_blocks, -1)
        first = jnp.where(entry >= 0, entry % max_blocks, 0) * BLK
        for s in range(SEQS):
            count = jnp.where(owner == s, ctx_buf[s] - first, 0)
            bias[s, :, b * BLK : (b + 1) * BLK] = jnp.where(lane < count, 0.0, LOW)

    new_k[...] = jnp.zeros_like(new_k)
    new_v[...] = jnp.zeros_like(new_v)
    for u in range(STEPS):
        new_k[u * SEQS : (u + 1) * SEQS, :] = new_buf[0, u].astype(jnp.float32)
        new_v[u * SEQS : (u + 1) * SEQS, :] = new_buf[1, u].astype(jnp.float32)

    def stacked(ref):
        parts = [ref[:, g * HEAD_DIM : (g + 1) * HEAD_DIM] for g in range(KV_HEADS)]
        return jnp.concatenate(parts, axis=0).astype(jnp.bfloat16)

    own_q = q_own[...]
    score = lax.dot_general(own_q, stacked(new_k), NT, preferred_element_type=jnp.float32)
    row = me * rows + lax.broadcasted_iota(jnp.int32, score.shape, 0)
    col = lax.broadcasted_iota(jnp.int32, score.shape, 1)
    pair = col % PAIRS
    allowed = (
        (pair < STEPS * SEQS)
        & (col // PAIRS == row % HEADS // PER_KV)
        & (pair % SEQS == row // HEADS % SEQS)
        & (pair // SEQS <= row // (HEADS * SEQS))
    )
    score = jnp.where(allowed, score, LOW)
    own_top = score.max(-1, keepdims=True)
    weight = jnp.where(allowed, jnp.exp2((score - own_top) * EXP_SCALE), 0.0)
    own_den = weight.sum(-1, keepdims=True)
    own_num[...] = jnp.dot(
        weight.astype(jnp.bfloat16), stacked(new_v), preferred_element_type=jnp.float32
    )
    eye = lax.broadcasted_iota(jnp.int32, (rows, HEAD_DIM), 0) == lax.broadcasted_iota(
        jnp.int32, (rows, HEAD_DIM), 1
    )

    def as_row(column):
        return jnp.sum(jnp.where(eye, column, 0.0), axis=0, keepdims=True)

    def as_column(line):
        return jnp.sum(jnp.where(eye, line, 0.0), axis=1, keepdims=True)

    own_stat[0:1, :] = as_row(own_top)
    own_stat[1:2, :] = as_row(own_den)

    pltpu.make_async_copy(kv_buf, kv_buf, load_sem.at[0]).wait()
    def sent(count, n):
        together(q_slots, count, q_send.at[n], q_recv.at[0]).wait_send()

    if relay:
        pl.when(plane <= 1)(functools.partial(sent, 1, 0))
        for n, count in ((1, 4 * quarter), (2, 4 * quarter - 4)):
            pl.when(hub)(functools.partial(sent, count, n))
        pl.when(plane > 1)(functools.partial(sent, devices - 1, 0))
    else:
        sent(devices - 1, 0)
    for g in range(KV_HEADS):
        kt_buf[g] = kv_buf[0, g].T
    together(q_slots, devices - 1, q_send.at[0], q_recv.at[0]).wait_recv()

    if not whole_groups:
        for d in range(devices):
            q_flat[d * rows : (d + 1) * rows, :] = q_slots[d].astype(jnp.float32)

    def gather(g):
        for s in range(SEQS):
            for t in range(STEPS):
                at = ((t * SEQS + s) * KV_HEADS + g) * PER_KV
                if whole_groups:
                    d, off = at // rows, at % rows
                    q_heads[g, s * STEPS + t] = q_slots[place(d), off : off + PER_KV, :]
                else:
                    q_heads[g, s * STEPS + t] = q_flat[at : at + PER_KV, :].astype(jnp.bfloat16)

    last = devices - devices // 4

    def result_copy(src, dst, slot, late):
        return pltpu.make_async_remote_copy(
            src_ref=send_msg.at[src],
            dst_ref=recv_msg.at[slot],
            send_sem=r_send.at[0],
            recv_sem=r_recv.at[late],
            device_id={"inner": dst},
            device_id_type=MESH,
        )

    def send_to(d):
        k = 0
        for bit, move in flips:
            here = me // bit % 2
            k = k + bit * (1 - here if d & bit else here)
        own = me == d
        dst, slot = jnp.where(own, target(1), d), jnp.where(own, devices, me)
        result_copy(d, dst, slot, jnp.where(k >= last, 1, 0)).start()

    stat_row = (rows + 7) // 8 * 8
    deep = lax.broadcasted_iota(jnp.int32, (8, HEAD_DIM), 0)

    def put_stats(d, high, total):
        block = jnp.zeros((8, HEAD_DIM), jnp.float32)
        for n, line in enumerate((high, total)):
            for m in range(3):
                part = line.astype(jnp.bfloat16).astype(jnp.float32)
                block = jnp.where(deep == 3 * n + m, part, block)
                line = line - part
        send_msg[d, stat_row : stat_row + 8, :] = block.astype(jnp.bfloat16)

    def message(ref, slot):
        block = ref[slot, stat_row : stat_row + 8, :].astype(jnp.float32)
        high = block[0:1] + block[1:2] + block[2:3]
        total = block[3:4] + block[4:5] + block[5:6]
        return high, total, ref[slot, 0:rows, :]

    def scores(g):
        gather(g)
        score = jnp.dot(
            q_heads[g].reshape(SEQS * QUERY_ROWS, HEAD_DIM), kt_buf[g], preferred_element_type=jnp.float32
        )
        score = score.reshape(SEQS, STEPS, PER_KV, tokens) + bias[...][:, None]
        score_buf[g] = score
        return score.max(-1, keepdims=True)

    def finish(g, high):
        weight = jnp.exp2((score_buf[g] - high) * EXP_SCALE)
        total = weight.sum(-1, keepdims=True)
        mixed = jnp.dot(
            weight.astype(jnp.bfloat16).reshape(SEQS * QUERY_ROWS, tokens),
            kv_buf[1, g],
            preferred_element_type=jnp.float32,
        )
        for s in range(SEQS):
            for t in range(STEPS):
                at = ((t * SEQS + s) * KV_HEADS + g) * PER_KV
                lo = (s * STEPS + t) * PER_KV
                part = mixed[lo : lo + PER_KV]
                if whole_groups:
                    d, off = at // rows, at % rows
                    send_msg[d, off : off + PER_KV, :] = part.astype(jnp.bfloat16)
                    spot = lane == sub + off
                    for which, column in enumerate((high, total)):
                        lines[d, which] = jnp.where(spot, column[s, t], lines.get((d, which), 0.0))
                    filled[d] += PER_KV
                    if filled[d] == rows:
                        ready.append(d)
                        put_stats(d, *(lines[d, n].sum(0, keepdims=True) for n in range(2)))
                else:
                    acc[at : at + PER_KV, :] = part
                    top[at : at + PER_KV, :] = jnp.broadcast_to(high[s, t], part.shape)
                    den[at : at + PER_KV, :] = jnp.broadcast_to(total[s, t], part.shape)

    sub = lax.broadcasted_iota(jnp.int32, (PER_KV, BLK), 0)
    lines, filled, ready = {}, [0] * devices, []
    highs = {g: scores(g) for g in range(3)}
    for group, after in (((0, 1, 2), (3, 4, 5)), ((3, 4, 5), (6, 7)), ((6, 7), ())):
        for g in group:
            finish(g, highs[g])
        if early:
            for d in sorted(ready):
                if d < devices // 2 or group[-1] == KV_HEADS - 1:
                    send_to(d)
                    ready.remove(d)
        for g in after:
            highs[g] = scores(g)
    if not whole_groups:
        for d in range(devices):
            part = slice(d * rows, (d + 1) * rows)
            send_msg[d, 0:rows, :] = acc[part, :].astype(jnp.bfloat16)
            put_stats(d, as_row(top[part, :]), as_row(den[part, :]))
    if not early:
        for k in far:
            result_copy(target(k), target(k), me, int(k >= last)).start()

    def merge(parts):
        high = functools.reduce(jnp.maximum, [top for top, _, _ in parts])
        scales = [jnp.exp2((top - high) * EXP_SCALE) for top, _, _ in parts]
        total = functools.reduce(jnp.add, [a * den for a, (_, den, _) in zip(scales, parts)])
        return high, scales, total

    def weighted(scales, parts):
        terms = [as_column(a) * num.astype(jnp.float32) for a, (_, _, num) in zip(scales, parts)]
        return functools.reduce(jnp.add, terms)

    spare = 1 if early else 0
    together(recv_msg, last - 1 + spare, r_send.at[0], r_recv.at[0]).wait_recv()
    parts = [
        (own_stat[0:1, :], own_stat[1:2, :], own_num[...]),
        message(send_msg, me),
    ] + [message(recv_msg, source(k)) for k in range(1, last)]
    high, scales, total = merge(parts)
    parts = [(high, total, weighted(scales, parts))]
    together(send_msg, devices - 1 + spare, r_send.at[0], r_recv.at[0]).wait_send()
    together(recv_msg, devices - last, r_send.at[0], r_recv.at[1]).wait_recv()
    parts += [message(recv_msg, source(k)) for k in range(last, devices)]
    high, scales, total = merge(parts)
    total = jnp.where(total > 0.0, total, 1.0)
    result = weighted([a / total for a in scales], parts)
    out_ref[...] = result.astype(out_ref.dtype)


def shards(queries, new_kv, cache_keys, cache_values, context_lengths, block_table):
    devices = lax.axis_size("inner")
    rows = queries.shape[0]
    every = rows * devices
    deep = ((rows + 7) // 8 * 8 + 8 + 15) // 16 * 16
    tokens, width = cache_keys.shape
    dma = pltpu.SemaphoreType.DMA
    f32, bf16 = jnp.float32, jnp.bfloat16
    call = pl.pallas_call(
        functools.partial(kernel, devices),
        out_shape=jax.ShapeDtypeStruct(queries.shape, queries.dtype),
        in_specs=[pl.BlockSpec(memory_space=pltpu.HBM)] * 6,
        out_specs=pl.BlockSpec(memory_space=pltpu.VMEM),
        scratch_shapes=[
            pltpu.VMEM((2, KV_HEADS, tokens, HEAD_DIM), bf16),
            pltpu.VMEM((KV_HEADS, HEAD_DIM, tokens), bf16),
            pltpu.VMEM(new_kv.shape, bf16),
            pltpu.SMEM(context_lengths.shape, jnp.int32),
            pltpu.SMEM(block_table.shape, jnp.int32),
            pltpu.VMEM((rows, HEAD_DIM), bf16),
            pltpu.VMEM((devices + 1, rows, HEAD_DIM), bf16),
            pltpu.VMEM((every, HEAD_DIM), f32),
            pltpu.VMEM((KV_HEADS, SEQS * STEPS, PER_KV, HEAD_DIM), bf16),
            pltpu.VMEM((SEQS, PER_KV, tokens), f32),
            pltpu.VMEM((PAIRS, width), f32),
            pltpu.VMEM((PAIRS, width), f32),
            pltpu.VMEM((rows, HEAD_DIM), f32),
            pltpu.VMEM((2, HEAD_DIM), f32),
            pltpu.VMEM((KV_HEADS, SEQS, STEPS, PER_KV, tokens), f32),
            pltpu.VMEM((every, HEAD_DIM), f32),
            pltpu.VMEM((every, HEAD_DIM), f32),
            pltpu.VMEM((every, HEAD_DIM), f32),
            pltpu.VMEM((devices, deep, HEAD_DIM), bf16),
            pltpu.VMEM((devices + 1, deep, HEAD_DIM), bf16),
            dma((1,)),
            dma((3,)),
            dma((2,)),
            dma((1,)),
            dma((2,)),
        ],
        compiler_params=pltpu.CompilerParams(
            collective_id=0, has_side_effects=True, vmem_limit_bytes=32 * 1024 * 1024
        ),
        name="paged_decode",
    )
    operands = (queries, new_kv, cache_keys, cache_values, context_lengths, block_table)
    return call(*(pltpu.with_memory_space_constraint(x, pltpu.HBM) for x in operands))


def solution(mesh):
    in_specs = (
        P(("parts", "inner"), None),
        P(None, None, "parts", None),
        P(("parts", "inner"), None),
        P(("parts", "inner"), None),
        P("parts"),
        P(("parts", "inner")),
    )
    out_specs = P(("parts", "inner"), None)
    return jax.shard_map(shards, mesh=mesh, in_specs=in_specs, out_specs=out_specs, check_vma=False)
```

```python
import functools
import math

import jax
import jax.numpy as jnp
from jax import lax
from jax.experimental import pallas as pl
from jax.experimental.pallas import tpu as pltpu
from jax.sharding import PartitionSpec as P

HEADS = 64
KV_HEADS = 8
HEAD_DIM = 128
SEQS = 2
BLK_DEV = 16
BLK = 128
STEPS = 3
PER_KV = HEADS // KV_HEADS
QUERY_ROWS = STEPS * PER_KV
PAIRS = 8
LOW = -1e30
EXP_SCALE = math.log2(math.e) / HEAD_DIM**0.5
MESH = pl.DeviceIdType.MESH
NT = (((1,), (1,)), ((), ()))


def kernel(
    devices,
    q_hbm, new_hbm, k_hbm, v_hbm, ctx_hbm, table_hbm,
    out_ref,
    kv_buf, kt_buf, new_buf, ctx_buf, table_buf,
    q_own, q_slots, q_flat, q_heads, bias,
    new_k, new_v, own_num, own_stat,
    score_buf, acc, top, den,
    send_msg, recv_msg,
    load_sem, q_send, q_recv, r_send, r_recv,
):
    me = lax.axis_index("inner")
    rows = q_hbm.shape[0]
    tokens = k_hbm.shape[0]
    max_blocks = 3 * BLK_DEV * devices // (2 * SEQS)

    power = devices & (devices - 1) == 0
    flips, bit = [], 1
    while bit < devices:
        flips.append((bit, bit * (1 - 2 * (me // bit % 2))))
        bit *= 2

    def target(k):
        if power:
            return me + sum(move for bit, move in flips if k & bit)
        return lax.rem(me + k, devices)

    def source(k):
        return target(k) if power else lax.rem(me + devices - k, devices)

    near = range(1, devices)
    far = range(devices - 1, 0, -1)
    load_q = pltpu.make_async_copy(q_hbm, q_own, q_send.at[0])
    load_q.start()
    small = (
        pltpu.make_async_copy(new_hbm, new_buf, q_send.at[1]),
        pltpu.make_async_copy(ctx_hbm, ctx_buf, q_send.at[2]),
        pltpu.make_async_copy(table_hbm, table_buf, r_send.at[0]),
    )
    for copy in small:
        copy.start()
    whole_groups = rows % PER_KV == 0
    early = power and whole_groups
    relay = early and devices >= 16
    quarter = devices // 4
    plane, column = me // quarter, me % quarter
    hub = plane == 1

    def place(d):
        return d % quarter * 4 + d // quarter if relay else d

    mine = place(me)
    barrier = pltpu.get_barrier_semaphore()

    def signal(semaphore, d):
        pl.semaphore_signal(semaphore, inc=1, device_id={"inner": d}, device_id_type=MESH)

    if relay:
        for d in [*range(quarter, 2 * quarter), *range(devices - 1, 2 * quarter - 1, -1), *range(quarter)]:
            pl.when(me != d if d >= quarter else me == d + quarter)(functools.partial(signal, barrier, d))
    else:
        for k in far:
            signal(barrier, target(k))

    loads = []
    for n, src in enumerate((k_hbm, v_hbm)):
        for g in range(KV_HEADS):
            part = pl.ds(g * HEAD_DIM, HEAD_DIM)
            loads.append(pltpu.make_async_copy(src.at[:, part], kv_buf.at[n, g], load_sem.at[0]))
    for copy in loads:
        copy.start()

    def query_copy(d, into):
        return pltpu.make_async_remote_copy(
            src_ref=q_own,
            dst_ref=q_slots.at[mine],
            send_sem=q_send.at[0],
            recv_sem=q_recv.at[into],
            device_id={"inner": d},
            device_id_type=MESH,
        )

    def pair_copy(d, out):
        pair = q_slots.at[pl.ds(column * 4, 2)]
        return pltpu.make_async_remote_copy(
            src_ref=pair,
            dst_ref=pair,
            send_sem=q_send.at[out],
            recv_sem=q_recv.at[0],
            device_id={"inner": d},
            device_id_type=MESH,
        )

    def others():
        return [(column + n) % quarter for n in range(1, quarter)]

    def together(ref, count, out_sem, in_sem):
        part = ref.at[pl.ds(0, count)]
        return pltpu.make_async_remote_copy(
            src_ref=part,
            dst_ref=part,
            send_sem=out_sem,
            recv_sem=in_sem,
            device_id={"inner": target(1)},
            device_id_type=MESH,
        )

    load_q.wait()
    for copy in small:
        copy.wait()
    q_slots[mine] = q_own[...]
    if relay:
        pl.semaphore_wait(barrier, jnp.where(plane == 0, 1, devices - 1))

        even = pltpu.make_async_copy(q_own, q_slots.at[devices], q_recv.at[jnp.where(hub, 0, 1)])
        even.start()

        @pl.when(plane == 0)
        def _():
            query_copy(me + quarter, 1).start()

        together(q_slots, 1, q_send.at[0], q_recv.at[1]).wait_recv()

        @pl.when(hub)
        def _():
            for d in [*range(3 * quarter, devices), *range(2 * quarter, 3 * quarter)]:
                pair_copy(d, 1).start()
            for d in others():
                pair_copy(quarter + d, 2).start()
            for d in others():
                pair_copy(d, 2).start()
            query_copy(column, 0).start()

        @pl.when(plane > 1)
        def _():
            for k in far:
                query_copy(target(k), 0).start()
    else:
        pl.semaphore_wait(barrier, devices - 1)
        for k in far:
            query_copy(target(k), 0).start()

    lane = lax.broadcasted_iota(jnp.int32, (8, BLK), 1)
    for b in range(tokens // BLK):
        entry = table_buf[b]
        owner = jnp.where(entry >= 0, entry // max_blocks, -1)
        first = jnp.where(entry >= 0, entry % max_blocks, 0) * BLK
        for s in range(SEQS):
            count = jnp.where(owner == s, ctx_buf[s] - first, 0)
            bias[s, :, b * BLK : (b + 1) * BLK] = jnp.where(lane < count, 0.0, LOW)

    new_k[...] = jnp.zeros_like(new_k)
    new_v[...] = jnp.zeros_like(new_v)
    for u in range(STEPS):
        new_k[u * SEQS : (u + 1) * SEQS, :] = new_buf[0, u].astype(jnp.float32)
        new_v[u * SEQS : (u + 1) * SEQS, :] = new_buf[1, u].astype(jnp.float32)

    def stacked(ref):
        parts = [ref[:, g * HEAD_DIM : (g + 1) * HEAD_DIM] for g in range(KV_HEADS)]
        return jnp.concatenate(parts, axis=0).astype(jnp.bfloat16)

    own_q = q_own[...]
    score = lax.dot_general(own_q, stacked(new_k), NT, preferred_element_type=jnp.float32)
    row = me * rows + lax.broadcasted_iota(jnp.int32, score.shape, 0)
    col = lax.broadcasted_iota(jnp.int32, score.shape, 1)
    pair = col % PAIRS
    allowed = (
        (pair < STEPS * SEQS)
        & (col // PAIRS == row % HEADS // PER_KV)
        & (pair % SEQS == row // HEADS % SEQS)
        & (pair // SEQS <= row // (HEADS * SEQS))
    )
    score = jnp.where(allowed, score, LOW)
    own_top = score.max(-1, keepdims=True)
    weight = jnp.where(allowed, jnp.exp2((score - own_top) * EXP_SCALE), 0.0)
    own_den = weight.sum(-1, keepdims=True)
    own_num[...] = jnp.dot(
        weight.astype(jnp.bfloat16), stacked(new_v), preferred_element_type=jnp.float32
    )
    eye = lax.broadcasted_iota(jnp.int32, (rows, HEAD_DIM), 0) == lax.broadcasted_iota(
        jnp.int32, (rows, HEAD_DIM), 1
    )

    def as_row(column):
        return jnp.sum(jnp.where(eye, column, 0.0), axis=0, keepdims=True)

    def as_column(line):
        return jnp.sum(jnp.where(eye, line, 0.0), axis=1, keepdims=True)

    own_stat[0:1, :] = as_row(own_top)
    own_stat[1:2, :] = as_row(own_den)

    pltpu.make_async_copy(kv_buf, kv_buf, load_sem.at[0]).wait()
    def sent(count, n):
        together(q_slots, count, q_send.at[n], q_recv.at[0]).wait_send()

    if relay:
        pl.when(plane <= 1)(functools.partial(sent, 1, 0))
        for n, count in ((1, 4 * quarter), (2, 4 * quarter - 4)):
            pl.when(hub)(functools.partial(sent, count, n))
        pl.when(plane > 1)(functools.partial(sent, devices - 1, 0))
    else:
        sent(devices - 1, 0)
    for g in range(KV_HEADS):
        kt_buf[g] = kv_buf[0, g].T
    together(q_slots, devices - 1, q_send.at[0], q_recv.at[0]).wait_recv()

    if not whole_groups:
        for d in range(devices):
            q_flat[d * rows : (d + 1) * rows, :] = q_slots[d].astype(jnp.float32)

    def gather(g):
        for s in range(SEQS):
            for t in range(STEPS):
                at = ((t * SEQS + s) * KV_HEADS + g) * PER_KV
                if whole_groups:
                    d, off = at // rows, at % rows
                    q_heads[g, s * STEPS + t] = q_slots[place(d), off : off + PER_KV, :]
                else:
                    q_heads[g, s * STEPS + t] = q_flat[at : at + PER_KV, :].astype(jnp.bfloat16)

    last = devices // 2

    def result_copy(src, dst, slot, late):
        return pltpu.make_async_remote_copy(
            src_ref=send_msg.at[src],
            dst_ref=recv_msg.at[slot],
            send_sem=r_send.at[0],
            recv_sem=r_recv.at[late],
            device_id={"inner": dst},
            device_id_type=MESH,
        )

    def send_to(d):
        k = 0
        for bit, move in flips:
            here = me // bit % 2
            k = k + bit * (1 - here if d & bit else here)
        own = me == d
        dst, slot = jnp.where(own, target(1), d), jnp.where(own, devices, me)
        result_copy(d, dst, slot, jnp.where(k >= last, 1, 0)).start()

    stat_row = (rows + 7) // 8 * 8
    deep = lax.broadcasted_iota(jnp.int32, (8, HEAD_DIM), 0)

    def put_stats(d, high, total):
        block = jnp.zeros((8, HEAD_DIM), jnp.float32)
        for n, line in enumerate((high, total)):
            for m in range(3):
                part = line.astype(jnp.bfloat16).astype(jnp.float32)
                block = jnp.where(deep == 3 * n + m, part, block)
                line = line - part
        send_msg[d, stat_row : stat_row + 8, :] = block.astype(jnp.bfloat16)

    def message(ref, slot):
        block = ref[slot, stat_row : stat_row + 8, :].astype(jnp.float32)
        high = block[0:1] + block[1:2] + block[2:3]
        total = block[3:4] + block[4:5] + block[5:6]
        return high, total, ref[slot, 0:rows, :]

    def scores(g):
        gather(g)
        score = jnp.dot(
            q_heads[g].reshape(SEQS * QUERY_ROWS, HEAD_DIM), kt_buf[g], preferred_element_type=jnp.float32
        )
        score = score.reshape(SEQS, STEPS, PER_KV, tokens) + bias[...][:, None]
        score_buf[g] = score
        return score.max(-1, keepdims=True)

    def finish(g, high):
        weight = jnp.exp2((score_buf[g] - high) * EXP_SCALE)
        total = weight.sum(-1, keepdims=True)
        mixed = jnp.dot(
            weight.astype(jnp.bfloat16).reshape(SEQS * QUERY_ROWS, tokens),
            kv_buf[1, g],
            preferred_element_type=jnp.float32,
        )
        for s in range(SEQS):
            for t in range(STEPS):
                at = ((t * SEQS + s) * KV_HEADS + g) * PER_KV
                lo = (s * STEPS + t) * PER_KV
                part = mixed[lo : lo + PER_KV]
                if whole_groups:
                    d, off = at // rows, at % rows
                    send_msg[d, off : off + PER_KV, :] = part.astype(jnp.bfloat16)
                    spot = lane == sub + off
                    for which, column in enumerate((high, total)):
                        lines[d, which] = jnp.where(spot, column[s, t], lines.get((d, which), 0.0))
                    filled[d] += PER_KV
                    if filled[d] == rows:
                        ready.append(d)
                        put_stats(d, *(lines[d, n].sum(0, keepdims=True) for n in range(2)))
                else:
                    acc[at : at + PER_KV, :] = part
                    top[at : at + PER_KV, :] = jnp.broadcast_to(high[s, t], part.shape)
                    den[at : at + PER_KV, :] = jnp.broadcast_to(total[s, t], part.shape)

    sub = lax.broadcasted_iota(jnp.int32, (PER_KV, BLK), 0)
    lines, filled, ready = {}, [0] * devices, []
    highs = {g: scores(g) for g in range(3)}
    for group, after in (((0, 1, 2), (3, 4, 5)), ((3, 4, 5), (6, 7)), ((6, 7), ())):
        for g in group:
            finish(g, highs[g])
        if early:
            for d in sorted(ready):
                if d < devices // 2 or group[-1] == KV_HEADS - 1:
                    send_to(d)
                    ready.remove(d)
        for g in after:
            highs[g] = scores(g)
    if not whole_groups:
        for d in range(devices):
            part = slice(d * rows, (d + 1) * rows)
            send_msg[d, 0:rows, :] = acc[part, :].astype(jnp.bfloat16)
            put_stats(d, as_row(top[part, :]), as_row(den[part, :]))
    if not early:
        for k in far:
            result_copy(target(k), target(k), me, int(k >= last)).start()

    def merge(parts):
        high = functools.reduce(jnp.maximum, [top for top, _, _ in parts])
        scales = [jnp.exp2((top - high) * EXP_SCALE) for top, _, _ in parts]
        total = functools.reduce(jnp.add, [a * den for a, (_, den, _) in zip(scales, parts)])
        return high, scales, total

    def weighted(scales, parts):
        terms = [as_column(a) * num.astype(jnp.float32) for a, (_, _, num) in zip(scales, parts)]
        return functools.reduce(jnp.add, terms)

    spare = 1 if early else 0
    together(recv_msg, last - 1 + spare, r_send.at[0], r_recv.at[0]).wait_recv()
    parts = [
        (own_stat[0:1, :], own_stat[1:2, :], own_num[...]),
        message(send_msg, me),
    ] + [message(recv_msg, source(k)) for k in range(1, last)]
    high, scales, total = merge(parts)
    parts = [(high, total, weighted(scales, parts))]
    together(send_msg, devices - 1 + spare, r_send.at[0], r_recv.at[0]).wait_send()
    together(recv_msg, devices - last, r_send.at[0], r_recv.at[1]).wait_recv()
    parts += [message(recv_msg, source(k)) for k in range(last, devices)]
    high, scales, total = merge(parts)
    total = jnp.where(total > 0.0, total, 1.0)
    result = weighted(scales, parts) * as_column(1.0 / total)
    out_ref[...] = result.astype(out_ref.dtype)


def shards(queries, new_kv, cache_keys, cache_values, context_lengths, block_table):
    devices = lax.axis_size("inner")
    rows = queries.shape[0]
    every = rows * devices
    deep = ((rows + 7) // 8 * 8 + 8 + 15) // 16 * 16
    tokens, width = cache_keys.shape
    dma = pltpu.SemaphoreType.DMA
    f32, bf16 = jnp.float32, jnp.bfloat16
    call = pl.pallas_call(
        functools.partial(kernel, devices),
        out_shape=jax.ShapeDtypeStruct(queries.shape, queries.dtype),
        in_specs=[pl.BlockSpec(memory_space=pltpu.HBM)] * 6,
        out_specs=pl.BlockSpec(memory_space=pltpu.VMEM),
        scratch_shapes=[
            pltpu.VMEM((2, KV_HEADS, tokens, HEAD_DIM), bf16),
            pltpu.VMEM((KV_HEADS, HEAD_DIM, tokens), bf16),
            pltpu.VMEM(new_kv.shape, bf16),
            pltpu.SMEM(context_lengths.shape, jnp.int32),
            pltpu.SMEM(block_table.shape, jnp.int32),
            pltpu.VMEM((rows, HEAD_DIM), bf16),
            pltpu.VMEM((devices + 1, rows, HEAD_DIM), bf16),
            pltpu.VMEM((every, HEAD_DIM), f32),
            pltpu.VMEM((KV_HEADS, SEQS * STEPS, PER_KV, HEAD_DIM), bf16),
            pltpu.VMEM((SEQS, PER_KV, tokens), f32),
            pltpu.VMEM((PAIRS, width), f32),
            pltpu.VMEM((PAIRS, width), f32),
            pltpu.VMEM((rows, HEAD_DIM), f32),
            pltpu.VMEM((2, HEAD_DIM), f32),
            pltpu.VMEM((KV_HEADS, SEQS, STEPS, PER_KV, tokens), f32),
            pltpu.VMEM((every, HEAD_DIM), f32),
            pltpu.VMEM((every, HEAD_DIM), f32),
            pltpu.VMEM((every, HEAD_DIM), f32),
            pltpu.VMEM((devices, deep, HEAD_DIM), bf16),
            pltpu.VMEM((devices + 1, deep, HEAD_DIM), bf16),
            dma((1,)),
            dma((3,)),
            dma((2,)),
            dma((1,)),
            dma((2,)),
        ],
        compiler_params=pltpu.CompilerParams(
            collective_id=0, has_side_effects=True, vmem_limit_bytes=32 * 1024 * 1024
        ),
        name="paged_decode",
    )
    operands = (queries, new_kv, cache_keys, cache_values, context_lengths, block_table)
    return call(*(pltpu.with_memory_space_constraint(x, pltpu.HBM) for x in operands))


def solution(mesh):
    in_specs = (
        P(("parts", "inner"), None),
        P(None, None, "parts", None),
        P(("parts", "inner"), None),
        P(("parts", "inner"), None),
        P("parts"),
        P(("parts", "inner")),
    )
    out_specs = P(("parts", "inner"), None)
    return jax.shard_map(shards, mesh=mesh, in_specs=in_specs, out_specs=out_specs, check_vma=False)
```

```python
import functools
import math

import jax
import jax.numpy as jnp
from jax import lax
from jax.experimental import pallas as pl
from jax.experimental.pallas import tpu as pltpu
from jax.sharding import PartitionSpec as P

HEADS = 64
KV_HEADS = 8
HEAD_DIM = 128
SEQS = 2
BLK_DEV = 16
BLK = 128
STEPS = 3
PER_KV = HEADS // KV_HEADS
QUERY_ROWS = STEPS * PER_KV
PAIRS = 8
LOW = -1e30
EXP_SCALE = math.log2(math.e) / HEAD_DIM**0.5
MESH = pl.DeviceIdType.MESH
NT = (((1,), (1,)), ((), ()))


def kernel(
    devices,
    q_hbm, new_hbm, k_hbm, v_hbm, ctx_hbm, table_hbm,
    out_ref,
    kv_buf, kt_buf, new_buf, ctx_buf, table_buf,
    q_own, q_slots, q_flat, q_heads, bias,
    new_k, new_v, own_num, own_stat,
    score_buf, acc, top, den,
    send_msg, recv_msg,
    load_sem, q_send, q_recv, r_send, r_recv,
):
    me = lax.axis_index("inner")
    rows = q_hbm.shape[0]
    tokens = k_hbm.shape[0]
    max_blocks = 3 * BLK_DEV * devices // (2 * SEQS)

    power = devices & (devices - 1) == 0
    flips, bit = [], 1
    while bit < devices:
        flips.append((bit, bit * (1 - 2 * (me // bit % 2))))
        bit *= 2

    def target(k):
        if power:
            return me + sum(move for bit, move in flips if k & bit)
        return lax.rem(me + k, devices)

    def source(k):
        return target(k) if power else lax.rem(me + devices - k, devices)

    near = range(1, devices)
    far = range(devices - 1, 0, -1)
    load_q = pltpu.make_async_copy(q_hbm, q_own, q_send.at[0])
    load_q.start()
    small = (
        pltpu.make_async_copy(new_hbm, new_buf, q_send.at[1]),
        pltpu.make_async_copy(ctx_hbm, ctx_buf, q_send.at[2]),
        pltpu.make_async_copy(table_hbm, table_buf, r_send.at[0]),
    )
    for copy in small:
        copy.start()
    whole_groups = rows % PER_KV == 0
    early = power and whole_groups
    relay = early and devices >= 16
    quarter = devices // 4
    plane, column = me // quarter, me % quarter
    hub = plane == 1

    def place(d):
        return d % quarter * 4 + d // quarter if relay else d

    mine = place(me)
    barrier = pltpu.get_barrier_semaphore()

    def signal(semaphore, d):
        pl.semaphore_signal(semaphore, inc=1, device_id={"inner": d}, device_id_type=MESH)

    if relay:
        for d in [*range(quarter, 2 * quarter), *range(devices - 1, 2 * quarter - 1, -1), *range(quarter)]:
            pl.when(me != d if d >= quarter else me == d + quarter)(functools.partial(signal, barrier, d))
    else:
        for k in far:
            signal(barrier, target(k))

    loads = []
    for n, src in enumerate((k_hbm, v_hbm)):
        for g in range(KV_HEADS):
            part = pl.ds(g * HEAD_DIM, HEAD_DIM)
            loads.append(pltpu.make_async_copy(src.at[:, part], kv_buf.at[n, g], load_sem.at[0]))
    for copy in loads:
        copy.start()

    def query_copy(d, into):
        return pltpu.make_async_remote_copy(
            src_ref=q_own,
            dst_ref=q_slots.at[mine],
            send_sem=q_send.at[0],
            recv_sem=q_recv.at[into],
            device_id={"inner": d},
            device_id_type=MESH,
        )

    def pair_copy(d, out):
        pair = q_slots.at[pl.ds(column * 4, 2)]
        return pltpu.make_async_remote_copy(
            src_ref=pair,
            dst_ref=pair,
            send_sem=q_send.at[out],
            recv_sem=q_recv.at[0],
            device_id={"inner": d},
            device_id_type=MESH,
        )

    def others():
        return [(column + n) % quarter for n in range(1, quarter)]

    def together(ref, count, out_sem, in_sem):
        part = ref.at[pl.ds(0, count)]
        return pltpu.make_async_remote_copy(
            src_ref=part,
            dst_ref=part,
            send_sem=out_sem,
            recv_sem=in_sem,
            device_id={"inner": target(1)},
            device_id_type=MESH,
        )

    load_q.wait()
    for copy in small:
        copy.wait()
    q_slots[mine] = q_own[...]
    if relay:
        pl.semaphore_wait(barrier, jnp.where(plane == 0, 1, devices - 1))

        even = pltpu.make_async_copy(q_own, q_slots.at[devices], q_recv.at[jnp.where(hub, 0, 1)])
        even.start()

        @pl.when(plane == 0)
        def _():
            query_copy(me + quarter, 1).start()

        together(q_slots, 1, q_send.at[0], q_recv.at[1]).wait_recv()

        @pl.when(hub)
        def _():
            for d in [*range(3 * quarter, devices), *range(2 * quarter, 3 * quarter)]:
                pair_copy(d, 1).start()
            for d in others():
                pair_copy(d, 2).start()
            for d in others():
                pair_copy(quarter + d, 2).start()
            query_copy(column, 0).start()

        @pl.when(plane > 1)
        def _():
            for k in far:
                query_copy(target(k), 0).start()
    else:
        pl.semaphore_wait(barrier, devices - 1)
        for k in far:
            query_copy(target(k), 0).start()

    lane = lax.broadcasted_iota(jnp.int32, (8, BLK), 1)
    for b in range(tokens // BLK):
        entry = table_buf[b]
        owner = jnp.where(entry >= 0, entry // max_blocks, -1)
        first = jnp.where(entry >= 0, entry % max_blocks, 0) * BLK
        for s in range(SEQS):
            count = jnp.where(owner == s, ctx_buf[s] - first, 0)
            bias[s, :, b * BLK : (b + 1) * BLK] = jnp.where(lane < count, 0.0, LOW)

    new_k[...] = jnp.zeros_like(new_k)
    new_v[...] = jnp.zeros_like(new_v)
    for u in range(STEPS):
        new_k[u * SEQS : (u + 1) * SEQS, :] = new_buf[0, u].astype(jnp.float32)
        new_v[u * SEQS : (u + 1) * SEQS, :] = new_buf[1, u].astype(jnp.float32)

    def stacked(ref):
        parts = [ref[:, g * HEAD_DIM : (g + 1) * HEAD_DIM] for g in range(KV_HEADS)]
        return jnp.concatenate(parts, axis=0).astype(jnp.bfloat16)

    own_q = q_own[...]
    score = lax.dot_general(own_q, stacked(new_k), NT, preferred_element_type=jnp.float32)
    row = me * rows + lax.broadcasted_iota(jnp.int32, score.shape, 0)
    col = lax.broadcasted_iota(jnp.int32, score.shape, 1)
    pair = col % PAIRS
    allowed = (
        (pair < STEPS * SEQS)
        & (col // PAIRS == row % HEADS // PER_KV)
        & (pair % SEQS == row // HEADS % SEQS)
        & (pair // SEQS <= row // (HEADS * SEQS))
    )
    score = jnp.where(allowed, score, LOW)
    own_top = score.max(-1, keepdims=True)
    weight = jnp.where(allowed, jnp.exp2((score - own_top) * EXP_SCALE), 0.0)
    own_den = weight.sum(-1, keepdims=True)
    own_num[...] = jnp.dot(
        weight.astype(jnp.bfloat16), stacked(new_v), preferred_element_type=jnp.float32
    )
    eye = lax.broadcasted_iota(jnp.int32, (rows, HEAD_DIM), 0) == lax.broadcasted_iota(
        jnp.int32, (rows, HEAD_DIM), 1
    )

    def as_row(column):
        return jnp.sum(jnp.where(eye, column, 0.0), axis=0, keepdims=True)

    def as_column(line):
        return jnp.sum(jnp.where(eye, line, 0.0), axis=1, keepdims=True)

    own_stat[0:1, :] = as_row(own_top)
    own_stat[1:2, :] = as_row(own_den)

    pltpu.make_async_copy(kv_buf, kv_buf, load_sem.at[0]).wait()
    def sent(count, n):
        together(q_slots, count, q_send.at[n], q_recv.at[0]).wait_send()

    if relay:
        pl.when(plane <= 1)(functools.partial(sent, 1, 0))
        for n, count in ((1, 4 * quarter), (2, 4 * quarter - 4)):
            pl.when(hub)(functools.partial(sent, count, n))
        pl.when(plane > 1)(functools.partial(sent, devices - 1, 0))
    else:
        sent(devices - 1, 0)
    for g in range(KV_HEADS):
        kt_buf[g] = kv_buf[0, g].T
    together(q_slots, devices - 1, q_send.at[0], q_recv.at[0]).wait_recv()

    if not whole_groups:
        for d in range(devices):
            q_flat[d * rows : (d + 1) * rows, :] = q_slots[d].astype(jnp.float32)

    def gather(g):
        for s in range(SEQS):
            for t in range(STEPS):
                at = ((t * SEQS + s) * KV_HEADS + g) * PER_KV
                if whole_groups:
                    d, off = at // rows, at % rows
                    q_heads[g, s * STEPS + t] = q_slots[place(d), off : off + PER_KV, :]
                else:
                    q_heads[g, s * STEPS + t] = q_flat[at : at + PER_KV, :].astype(jnp.bfloat16)

    last = devices // 2

    def result_copy(src, dst, slot, late):
        return pltpu.make_async_remote_copy(
            src_ref=send_msg.at[src],
            dst_ref=recv_msg.at[slot],
            send_sem=r_send.at[0],
            recv_sem=r_recv.at[late],
            device_id={"inner": dst},
            device_id_type=MESH,
        )

    def send_to(d):
        k = 0
        for bit, move in flips:
            here = me // bit % 2
            k = k + bit * (1 - here if d & bit else here)
        own = me == d
        dst, slot = jnp.where(own, target(1), d), jnp.where(own, devices, me)
        result_copy(d, dst, slot, jnp.where(k >= last, 1, 0)).start()

    stat_row = (rows + 7) // 8 * 8
    deep = lax.broadcasted_iota(jnp.int32, (8, HEAD_DIM), 0)

    def put_stats(d, high, total):
        block = jnp.zeros((8, HEAD_DIM), jnp.float32)
        for n, line in enumerate((high, total)):
            for m in range(3):
                part = line.astype(jnp.bfloat16).astype(jnp.float32)
                block = jnp.where(deep == 3 * n + m, part, block)
                line = line - part
        send_msg[d, stat_row : stat_row + 8, :] = block.astype(jnp.bfloat16)

    def message(ref, slot):
        block = ref[slot, stat_row : stat_row + 8, :].astype(jnp.float32)
        high = block[0:1] + block[1:2] + block[2:3]
        total = block[3:4] + block[4:5] + block[5:6]
        return high, total, ref[slot, 0:rows, :]

    def scores(g):
        gather(g)
        score = jnp.dot(
            q_heads[g].reshape(SEQS * QUERY_ROWS, HEAD_DIM), kt_buf[g], preferred_element_type=jnp.float32
        )
        score = score.reshape(SEQS, STEPS, PER_KV, tokens) + bias[...][:, None]
        score_buf[g] = score
        return score.max(-1, keepdims=True)

    def finish(g, high):
        weight = jnp.exp2((score_buf[g] - high) * EXP_SCALE)
        total = weight.sum(-1, keepdims=True)
        mixed = jnp.dot(
            weight.astype(jnp.bfloat16).reshape(SEQS * QUERY_ROWS, tokens),
            kv_buf[1, g],
            preferred_element_type=jnp.float32,
        )
        for s in range(SEQS):
            for t in range(STEPS):
                at = ((t * SEQS + s) * KV_HEADS + g) * PER_KV
                lo = (s * STEPS + t) * PER_KV
                part = mixed[lo : lo + PER_KV]
                if whole_groups:
                    d, off = at // rows, at % rows
                    send_msg[d, off : off + PER_KV, :] = part.astype(jnp.bfloat16)
                    spot = lane == sub + off
                    for which, column in enumerate((high, total)):
                        lines[d, which] = jnp.where(spot, column[s, t], lines.get((d, which), 0.0))
                    filled[d] += PER_KV
                    if filled[d] == rows:
                        ready.append(d)
                        put_stats(d, *(lines[d, n].sum(0, keepdims=True) for n in range(2)))
                else:
                    acc[at : at + PER_KV, :] = part
                    top[at : at + PER_KV, :] = jnp.broadcast_to(high[s, t], part.shape)
                    den[at : at + PER_KV, :] = jnp.broadcast_to(total[s, t], part.shape)

    sub = lax.broadcasted_iota(jnp.int32, (PER_KV, BLK), 0)
    lines, filled, ready = {}, [0] * devices, []
    highs = {g: scores(g) for g in range(3)}
    for group, after in (((0, 1, 2), (3, 4, 5)), ((3, 4, 5), (6, 7)), ((6, 7), ())):
        for g in group:
            finish(g, highs[g])
        if early:
            for d in sorted(ready):
                if d < devices // 2 or group[-1] == KV_HEADS - 1:
                    send_to(d)
                    ready.remove(d)
        for g in after:
            highs[g] = scores(g)
    if not whole_groups:
        for d in range(devices):
            part = slice(d * rows, (d + 1) * rows)
            send_msg[d, 0:rows, :] = acc[part, :].astype(jnp.bfloat16)
            put_stats(d, as_row(top[part, :]), as_row(den[part, :]))
    if not early:
        for k in far:
            result_copy(target(k), target(k), me, int(k >= last)).start()

    def merge(parts):
        high = functools.reduce(jnp.maximum, [top for top, _, _ in parts])
        scales = [jnp.exp2((top - high) * EXP_SCALE) for top, _, _ in parts]
        total = functools.reduce(jnp.add, [a * den for a, (_, den, _) in zip(scales, parts)])
        return high, scales, total

    def weighted(scales, parts):
        terms = [as_column(a) * num.astype(jnp.float32) for a, (_, _, num) in zip(scales, parts)]
        return functools.reduce(jnp.add, terms)

    spare = 1 if early else 0
    together(recv_msg, last - 1 + spare, r_send.at[0], r_recv.at[0]).wait_recv()
    parts = [
        (own_stat[0:1, :], own_stat[1:2, :], own_num[...]),
        message(send_msg, me),
    ] + [message(recv_msg, source(k)) for k in range(1, last)]
    high, scales, total = merge(parts)
    parts = [(high, total, weighted(scales, parts))]
    together(send_msg, devices - 1 + spare, r_send.at[0], r_recv.at[0]).wait_send()
    together(recv_msg, devices - last, r_send.at[0], r_recv.at[1]).wait_recv()
    parts += [message(recv_msg, source(k)) for k in range(last, devices)]
    high, scales, total = merge(parts)
    total = jnp.where(total > 0.0, total, 1.0)
    result = weighted(scales, parts) * as_column(1.0 / total)
    out_ref[...] = result.astype(out_ref.dtype)


def shards(queries, new_kv, cache_keys, cache_values, context_lengths, block_table):
    devices = lax.axis_size("inner")
    rows = queries.shape[0]
    every = rows * devices
    deep = ((rows + 7) // 8 * 8 + 8 + 15) // 16 * 16
    tokens, width = cache_keys.shape
    dma = pltpu.SemaphoreType.DMA
    f32, bf16 = jnp.float32, jnp.bfloat16
    call = pl.pallas_call(
        functools.partial(kernel, devices),
        out_shape=jax.ShapeDtypeStruct(queries.shape, queries.dtype),
        in_specs=[pl.BlockSpec(memory_space=pltpu.HBM)] * 6,
        out_specs=pl.BlockSpec(memory_space=pltpu.VMEM),
        scratch_shapes=[
            pltpu.VMEM((2, KV_HEADS, tokens, HEAD_DIM), bf16),
            pltpu.VMEM((KV_HEADS, HEAD_DIM, tokens), bf16),
            pltpu.VMEM(new_kv.shape, bf16),
            pltpu.SMEM(context_lengths.shape, jnp.int32),
            pltpu.SMEM(block_table.shape, jnp.int32),
            pltpu.VMEM((rows, HEAD_DIM), bf16),
            pltpu.VMEM((devices + 1, rows, HEAD_DIM), bf16),
            pltpu.VMEM((every, HEAD_DIM), f32),
            pltpu.VMEM((KV_HEADS, SEQS * STEPS, PER_KV, HEAD_DIM), bf16),
            pltpu.VMEM((SEQS, PER_KV, tokens), f32),
            pltpu.VMEM((PAIRS, width), f32),
            pltpu.VMEM((PAIRS, width), f32),
            pltpu.VMEM((rows, HEAD_DIM), f32),
            pltpu.VMEM((2, HEAD_DIM), f32),
            pltpu.VMEM((KV_HEADS, SEQS, STEPS, PER_KV, tokens), f32),
            pltpu.VMEM((every, HEAD_DIM), f32),
            pltpu.VMEM((every, HEAD_DIM), f32),
            pltpu.VMEM((every, HEAD_DIM), f32),
            pltpu.VMEM((devices, deep, HEAD_DIM), bf16),
            pltpu.VMEM((devices + 1, deep, HEAD_DIM), bf16),
            dma((1,)),
            dma((3,)),
            dma((2,)),
            dma((1,)),
            dma((2,)),
        ],
        compiler_params=pltpu.CompilerParams(
            collective_id=0, has_side_effects=True, vmem_limit_bytes=32 * 1024 * 1024
        ),
        name="paged_decode",
    )
    operands = (queries, new_kv, cache_keys, cache_values, context_lengths, block_table)
    return call(*(pltpu.with_memory_space_constraint(x, pltpu.HBM) for x in operands))


def solution(mesh):
    in_specs = (
        P(("parts", "inner"), None),
        P(None, None, "parts", None),
        P(("parts", "inner"), None),
        P(("parts", "inner"), None),
        P("parts"),
        P(("parts", "inner")),
    )
    out_specs = P(("parts", "inner"), None)
    return jax.shard_map(shards, mesh=mesh, in_specs=in_specs, out_specs=out_specs, check_vma=False)
```

```python
import functools
import math

import jax
import jax.numpy as jnp
from jax import lax
from jax.experimental import pallas as pl
from jax.experimental.pallas import tpu as pltpu
from jax.sharding import PartitionSpec as P

HEADS = 64
KV_HEADS = 8
HEAD_DIM = 128
SEQS = 2
BLK_DEV = 16
BLK = 128
STEPS = 3
PER_KV = HEADS // KV_HEADS
QUERY_ROWS = STEPS * PER_KV
PAIRS = 8
LOW = -1e30
EXP_SCALE = math.log2(math.e) / HEAD_DIM**0.5
MESH = pl.DeviceIdType.MESH
NT = (((1,), (1,)), ((), ()))


def kernel(
    devices,
    q_hbm, new_hbm, k_hbm, v_hbm, ctx_hbm, table_hbm,
    out_ref,
    kv_buf, kt_buf, new_buf, ctx_buf, table_buf,
    q_own, q_slots, q_flat, q_heads, bias,
    new_k, new_v, own_num, own_stat,
    score_buf, acc, top, den,
    send_msg, recv_msg,
    load_sem, q_send, q_recv, r_send, r_recv,
):
    me = lax.axis_index("inner")
    rows = q_hbm.shape[0]
    tokens = k_hbm.shape[0]
    max_blocks = 3 * BLK_DEV * devices // (2 * SEQS)

    power = devices & (devices - 1) == 0
    flips, bit = [], 1
    while bit < devices:
        flips.append((bit, bit * (1 - 2 * (me // bit % 2))))
        bit *= 2

    def target(k):
        if power:
            return me + sum(move for bit, move in flips if k & bit)
        return lax.rem(me + k, devices)

    def source(k):
        return target(k) if power else lax.rem(me + devices - k, devices)

    near = range(1, devices)
    far = range(devices - 1, 0, -1)
    load_q = pltpu.make_async_copy(q_hbm, q_own, q_send.at[0])
    load_q.start()
    small = (
        pltpu.make_async_copy(new_hbm, new_buf, q_send.at[1]),
        pltpu.make_async_copy(ctx_hbm, ctx_buf, q_send.at[2]),
        pltpu.make_async_copy(table_hbm, table_buf, r_send.at[0]),
    )
    for copy in small:
        copy.start()
    whole_groups = rows % PER_KV == 0
    early = power and whole_groups
    relay = early and devices >= 16
    quarter = devices // 4
    plane, column = me // quarter, me % quarter
    hub = plane == 1

    def place(d):
        return d % quarter * 4 + d // quarter if relay else d

    mine = place(me)
    barrier = pltpu.get_barrier_semaphore()

    def signal(semaphore, d):
        pl.semaphore_signal(semaphore, inc=1, device_id={"inner": d}, device_id_type=MESH)

    if relay:
        for d in [*range(quarter, 2 * quarter), *range(devices - 1, 2 * quarter - 1, -1), *range(quarter)]:
            pl.when(me != d if d >= quarter else me == d + quarter)(functools.partial(signal, barrier, d))
    else:
        for k in far:
            signal(barrier, target(k))

    loads = []
    for n, src in enumerate((k_hbm, v_hbm)):
        for g in range(KV_HEADS):
            part = pl.ds(g * HEAD_DIM, HEAD_DIM)
            loads.append(pltpu.make_async_copy(src.at[:, part], kv_buf.at[n, g], load_sem.at[0]))
    for copy in loads:
        copy.start()

    def query_copy(d, into):
        return pltpu.make_async_remote_copy(
            src_ref=q_own,
            dst_ref=q_slots.at[mine],
            send_sem=q_send.at[0],
            recv_sem=q_recv.at[into],
            device_id={"inner": d},
            device_id_type=MESH,
        )

    def pair_copy(d, out):
        pair = q_slots.at[pl.ds(column * 4, 2)]
        return pltpu.make_async_remote_copy(
            src_ref=pair,
            dst_ref=pair,
            send_sem=q_send.at[out],
            recv_sem=q_recv.at[0],
            device_id={"inner": d},
            device_id_type=MESH,
        )

    def others():
        return [(column + n) % quarter for n in range(1, quarter)]

    def together(ref, count, out_sem, in_sem):
        part = ref.at[pl.ds(0, count)]
        return pltpu.make_async_remote_copy(
            src_ref=part,
            dst_ref=part,
            send_sem=out_sem,
            recv_sem=in_sem,
            device_id={"inner": target(1)},
            device_id_type=MESH,
        )

    load_q.wait()
    for copy in small:
        copy.wait()
    q_slots[mine] = q_own[...]
    if relay:
        pl.semaphore_wait(barrier, jnp.where(plane == 0, 1, devices - 1))

        even = pltpu.make_async_copy(q_own, q_slots.at[devices], q_recv.at[jnp.where(hub, 0, 1)])
        even.start()

        @pl.when(plane == 0)
        def _():
            query_copy(me + quarter, 1).start()

        together(q_slots, 1, q_send.at[0], q_recv.at[1]).wait_recv()

        @pl.when(hub)
        def _():
            for d in [*range(3 * quarter, devices), *range(2 * quarter, 3 * quarter)]:
                pair_copy(d, 1).start()
            for d in others():
                pair_copy(quarter + d, 2).start()
            for d in others():
                pair_copy(d, 2).start()
            query_copy(column, 0).start()

        @pl.when(plane > 1)
        def _():
            for k in far:
                query_copy(target(k), 0).start()
    else:
        pl.semaphore_wait(barrier, devices - 1)
        for k in far:
            query_copy(target(k), 0).start()

    lane = lax.broadcasted_iota(jnp.int32, (8, BLK), 1)
    for b in range(tokens // BLK):
        entry = table_buf[b]
        owner = jnp.where(entry >= 0, entry // max_blocks, -1)
        first = jnp.where(entry >= 0, entry % max_blocks, 0) * BLK
        for s in range(SEQS):
            count = jnp.where(owner == s, ctx_buf[s] - first, 0)
            bias[s, :, b * BLK : (b + 1) * BLK] = jnp.where(lane < count, 0.0, LOW)

    new_k[...] = jnp.zeros_like(new_k)
    new_v[...] = jnp.zeros_like(new_v)
    for u in range(STEPS):
        new_k[u * SEQS : (u + 1) * SEQS, :] = new_buf[0, u].astype(jnp.float32)
        new_v[u * SEQS : (u + 1) * SEQS, :] = new_buf[1, u].astype(jnp.float32)

    def stacked(ref):
        parts = [ref[:, g * HEAD_DIM : (g + 1) * HEAD_DIM] for g in range(KV_HEADS)]
        return jnp.concatenate(parts, axis=0).astype(jnp.bfloat16)

    own_q = q_own[...]
    score = lax.dot_general(own_q, stacked(new_k), NT, preferred_element_type=jnp.float32)
    row = me * rows + lax.broadcasted_iota(jnp.int32, score.shape, 0)
    col = lax.broadcasted_iota(jnp.int32, score.shape, 1)
    pair = col % PAIRS
    allowed = (
        (pair < STEPS * SEQS)
        & (col // PAIRS == row % HEADS // PER_KV)
        & (pair % SEQS == row // HEADS % SEQS)
        & (pair // SEQS <= row // (HEADS * SEQS))
    )
    score = jnp.where(allowed, score, LOW)
    own_top = score.max(-1, keepdims=True)
    weight = jnp.where(allowed, jnp.exp2((score - own_top) * EXP_SCALE), 0.0)
    own_den = weight.sum(-1, keepdims=True)
    own_num[...] = jnp.dot(
        weight.astype(jnp.bfloat16), stacked(new_v), preferred_element_type=jnp.float32
    )
    eye = lax.broadcasted_iota(jnp.int32, (rows, HEAD_DIM), 0) == lax.broadcasted_iota(
        jnp.int32, (rows, HEAD_DIM), 1
    )

    def as_row(column):
        return jnp.sum(jnp.where(eye, column, 0.0), axis=0, keepdims=True)

    def as_column(line):
        return jnp.sum(jnp.where(eye, line, 0.0), axis=1, keepdims=True)

    own_stat[0:1, :] = as_row(own_top)
    own_stat[1:2, :] = as_row(own_den)

    pltpu.make_async_copy(kv_buf, kv_buf, load_sem.at[0]).wait()
    def sent(count, n):
        together(q_slots, count, q_send.at[n], q_recv.at[0]).wait_send()

    if relay:
        pl.when(plane <= 1)(functools.partial(sent, 1, 0))
        for n, count in ((1, 4 * quarter), (2, 4 * quarter - 4)):
            pl.when(hub)(functools.partial(sent, count, n))
        pl.when(plane > 1)(functools.partial(sent, devices - 1, 0))
    else:
        sent(devices - 1, 0)
    for g in range(KV_HEADS):
        kt_buf[g] = kv_buf[0, g].T
    together(q_slots, devices - 1, q_send.at[0], q_recv.at[0]).wait_recv()

    if not whole_groups:
        for d in range(devices):
            q_flat[d * rows : (d + 1) * rows, :] = q_slots[d].astype(jnp.float32)

    def gather(g):
        for s in range(SEQS):
            for t in range(STEPS):
                at = ((t * SEQS + s) * KV_HEADS + g) * PER_KV
                if whole_groups:
                    d, off = at // rows, at % rows
                    q_heads[g, s * STEPS + t] = q_slots[place(d), off : off + PER_KV, :]
                else:
                    q_heads[g, s * STEPS + t] = q_flat[at : at + PER_KV, :].astype(jnp.bfloat16)

    last = devices // 2

    def result_copy(src, dst, slot, late):
        return pltpu.make_async_remote_copy(
            src_ref=send_msg.at[src],
            dst_ref=recv_msg.at[slot],
            send_sem=r_send.at[0],
            recv_sem=r_recv.at[late],
            device_id={"inner": dst},
            device_id_type=MESH,
        )

    def send_to(d):
        k = 0
        for bit, move in flips:
            here = me // bit % 2
            k = k + bit * (1 - here if d & bit else here)
        own = me == d
        dst, slot = jnp.where(own, target(1), d), jnp.where(own, devices, me)
        result_copy(d, dst, slot, jnp.where(k >= last, 1, 0)).start()

    stat_row = (rows + 7) // 8 * 8
    deep = lax.broadcasted_iota(jnp.int32, (8, HEAD_DIM), 0)

    def put_stats(d, high, total):
        block = jnp.zeros((8, HEAD_DIM), jnp.float32)
        for n, line in enumerate((high, total)):
            for m in range(3):
                part = line.astype(jnp.bfloat16).astype(jnp.float32)
                block = jnp.where(deep == 3 * n + m, part, block)
                line = line - part
        send_msg[d, stat_row : stat_row + 8, :] = block.astype(jnp.bfloat16)

    def message(ref, slot):
        block = ref[slot, stat_row : stat_row + 8, :].astype(jnp.float32)
        high = block[0:1] + block[1:2] + block[2:3]
        total = block[3:4] + block[4:5] + block[5:6]
        return high, total, ref[slot, 0:rows, :]

    def scores(g):
        gather(g)
        score = jnp.dot(
            q_heads[g].reshape(SEQS * QUERY_ROWS, HEAD_DIM), kt_buf[g], preferred_element_type=jnp.float32
        )
        score = score.reshape(SEQS, STEPS, PER_KV, tokens) + bias[...][:, None]
        score_buf[g] = score
        return score.max(-1, keepdims=True)

    def finish(g, high):
        weight = jnp.exp2((score_buf[g] - high) * EXP_SCALE)
        total = weight.sum(-1, keepdims=True)
        mixed = jnp.dot(
            weight.astype(jnp.bfloat16).reshape(SEQS * QUERY_ROWS, tokens),
            kv_buf[1, g],
            preferred_element_type=jnp.float32,
        )
        for s in range(SEQS):
            for t in range(STEPS):
                at = ((t * SEQS + s) * KV_HEADS + g) * PER_KV
                lo = (s * STEPS + t) * PER_KV
                part = mixed[lo : lo + PER_KV]
                if whole_groups:
                    d, off = at // rows, at % rows
                    send_msg[d, off : off + PER_KV, :] = part.astype(jnp.bfloat16)
                    spot = lane == sub + off
                    for which, column in enumerate((high, total)):
                        lines[d, which] = jnp.where(spot, column[s, t], lines.get((d, which), 0.0))
                    filled[d] += PER_KV
                    if filled[d] == rows:
                        ready.append(d)
                        put_stats(d, *(lines[d, n].sum(0, keepdims=True) for n in range(2)))
                else:
                    acc[at : at + PER_KV, :] = part
                    top[at : at + PER_KV, :] = jnp.broadcast_to(high[s, t], part.shape)
                    den[at : at + PER_KV, :] = jnp.broadcast_to(total[s, t], part.shape)

    sub = lax.broadcasted_iota(jnp.int32, (PER_KV, BLK), 0)
    lines, filled, ready = {}, [0] * devices, []
    highs = {g: scores(g) for g in range(4)}
    for group, after in (((0, 1, 2), (4, 5)), ((3, 4, 5), (6, 7)), ((6, 7), ())):
        for g in group:
            finish(g, highs[g])
        if early:
            for d in sorted(ready):
                if d < devices // 2 or group[-1] == KV_HEADS - 1:
                    send_to(d)
                    ready.remove(d)
        for g in after:
            highs[g] = scores(g)
    if not whole_groups:
        for d in range(devices):
            part = slice(d * rows, (d + 1) * rows)
            send_msg[d, 0:rows, :] = acc[part, :].astype(jnp.bfloat16)
            put_stats(d, as_row(top[part, :]), as_row(den[part, :]))
    if not early:
        for k in far:
            result_copy(target(k), target(k), me, int(k >= last)).start()

    def merge(parts):
        high = functools.reduce(jnp.maximum, [top for top, _, _ in parts])
        scales = [jnp.exp2((top - high) * EXP_SCALE) for top, _, _ in parts]
        total = functools.reduce(jnp.add, [a * den for a, (_, den, _) in zip(scales, parts)])
        return high, scales, total

    def weighted(scales, parts):
        terms = [as_column(a) * num.astype(jnp.float32) for a, (_, _, num) in zip(scales, parts)]
        return functools.reduce(jnp.add, terms)

    spare = 1 if early else 0
    together(recv_msg, last - 1 + spare, r_send.at[0], r_recv.at[0]).wait_recv()
    parts = [
        (own_stat[0:1, :], own_stat[1:2, :], own_num[...]),
        message(send_msg, me),
    ] + [message(recv_msg, source(k)) for k in range(1, last)]
    high, scales, total = merge(parts)
    parts = [(high, total, weighted(scales, parts))]
    together(send_msg, devices - 1 + spare, r_send.at[0], r_recv.at[0]).wait_send()
    together(recv_msg, devices - last, r_send.at[0], r_recv.at[1]).wait_recv()
    parts += [message(recv_msg, source(k)) for k in range(last, devices)]
    high, scales, total = merge(parts)
    total = jnp.where(total > 0.0, total, 1.0)
    result = weighted(scales, parts) * as_column(1.0 / total)
    out_ref[...] = result.astype(out_ref.dtype)


def shards(queries, new_kv, cache_keys, cache_values, context_lengths, block_table):
    devices = lax.axis_size("inner")
    rows = queries.shape[0]
    every = rows * devices
    deep = ((rows + 7) // 8 * 8 + 8 + 15) // 16 * 16
    tokens, width = cache_keys.shape
    dma = pltpu.SemaphoreType.DMA
    f32, bf16 = jnp.float32, jnp.bfloat16
    call = pl.pallas_call(
        functools.partial(kernel, devices),
        out_shape=jax.ShapeDtypeStruct(queries.shape, queries.dtype),
        in_specs=[pl.BlockSpec(memory_space=pltpu.HBM)] * 6,
        out_specs=pl.BlockSpec(memory_space=pltpu.VMEM),
        scratch_shapes=[
            pltpu.VMEM((2, KV_HEADS, tokens, HEAD_DIM), bf16),
            pltpu.VMEM((KV_HEADS, HEAD_DIM, tokens), bf16),
            pltpu.VMEM(new_kv.shape, bf16),
            pltpu.SMEM(context_lengths.shape, jnp.int32),
            pltpu.SMEM(block_table.shape, jnp.int32),
            pltpu.VMEM((rows, HEAD_DIM), bf16),
            pltpu.VMEM((devices + 1, rows, HEAD_DIM), bf16),
            pltpu.VMEM((every, HEAD_DIM), f32),
            pltpu.VMEM((KV_HEADS, SEQS * STEPS, PER_KV, HEAD_DIM), bf16),
            pltpu.VMEM((SEQS, PER_KV, tokens), f32),
            pltpu.VMEM((PAIRS, width), f32),
            pltpu.VMEM((PAIRS, width), f32),
            pltpu.VMEM((rows, HEAD_DIM), f32),
            pltpu.VMEM((2, HEAD_DIM), f32),
            pltpu.VMEM((KV_HEADS, SEQS, STEPS, PER_KV, tokens), f32),
            pltpu.VMEM((every, HEAD_DIM), f32),
            pltpu.VMEM((every, HEAD_DIM), f32),
            pltpu.VMEM((every, HEAD_DIM), f32),
            pltpu.VMEM((devices, deep, HEAD_DIM), bf16),
            pltpu.VMEM((devices + 1, deep, HEAD_DIM), bf16),
            dma((1,)),
            dma((3,)),
            dma((2,)),
            dma((1,)),
            dma((2,)),
        ],
        compiler_params=pltpu.CompilerParams(
            collective_id=0, has_side_effects=True, vmem_limit_bytes=32 * 1024 * 1024
        ),
        name="paged_decode",
    )
    operands = (queries, new_kv, cache_keys, cache_values, context_lengths, block_table)
    return call(*(pltpu.with_memory_space_constraint(x, pltpu.HBM) for x in operands))


def solution(mesh):
    in_specs = (
        P(("parts", "inner"), None),
        P(None, None, "parts", None),
        P(("parts", "inner"), None),
        P(("parts", "inner"), None),
        P("parts"),
        P(("parts", "inner")),
    )
    out_specs = P(("parts", "inner"), None)
    return jax.shard_map(shards, mesh=mesh, in_specs=in_specs, out_specs=out_specs, check_vma=False)
```
